32 devices in a mesh: dp: 2 (over y), fsdp: 16 (over z, x, core).
Axes of the slice: x: 2, y: 2, z: 4, core: 2. Of those that a mesh axis runs over, the one named last changes fastest.
Arguments:
- tokens: bfloat16 [32768, 1024], P(('dp', 'fsdp')), may hold values from -12 to 12
- ln_gain: bfloat16 [1024], P(('dp', 'fsdp')), may hold values from 0.099609375 to 1.8984375
- ln_bias: bfloat16 [1024], P(('dp', 'fsdp')), may hold values from -1.75 to 1.75
- qkv_weight: bfloat16 [1024, 3072], P(('dp', 'fsdp')), may hold values from -0.1875 to 0.1875
- qkv_bias: bfloat16 [3072], P(('dp', 'fsdp')), may hold values from -1.75 to 1.75
- out_weight: bfloat16 [1024, 1024], P(('dp', 'fsdp')), may hold values from -0.75 to 0.75
- out_bias: bfloat16 [1024], P(('dp', 'fsdp')), may hold values from -1.75 to 1.75
- fc1_weight: bfloat16 [1024, 4096], P(('dp', 'fsdp')), may hold values from -0.1875 to 0.1875
- fc1_bias: bfloat16 [4096], P(('dp', 'fsdp')), may hold values from -3 to 3
- fc2_weight: bfloat16 [4096, 1024], P(('dp', 'fsdp')), may hold values from -0.09375 to 0.09375
- fc2_bias: bfloat16 [1024], P(('dp', 'fsdp')), may hold values from -1.75 to 1.75
- cotangent: float32 [32768, 1024], P(('dp', 'fsdp')), may hold values from -6 to 6
- doc_lengths: int32 [32, 4], P(('dp', 'fsdp')), may hold values from 1 to 512, 1024 in all within a row
- node_seeds: int32 [64, 64], replicated, may hold values from 0 to 1023
- node_weights: int32 [64], replicated, may hold values from 1 to 16
Outputs:
- output: float32 [32768, 1024], P(('dp', 'fsdp'))
- input_grad: float32 [32768, 1024], P(('dp', 'fsdp'))
- g_ln_gain: float32 [1024], P(('dp', 'fsdp'))
- g_ln_bias: float32 [1024], P(('dp', 'fsdp'))
- g_qkv_weight: float32 [1024, 3072], P(('dp', 'fsdp'))
- g_qkv_bias: float32 [3072], P(('dp', 'fsdp'))
- g_out_weight: float32 [1024, 1024], P(('dp', 'fsdp'))
- g_out_bias: float32 [1024], P(('dp', 'fsdp'))
- g_fc1_weight: float32 [1024, 4096], P(('dp', 'fsdp'))
- g_fc1_bias: float32 [4096], P(('dp', 'fsdp'))
- g_fc2_weight: float32 [4096, 1024], P(('dp', 'fsdp'))
- g_fc2_bias: float32 [1024], P(('dp', 'fsdp'))
The draws below stay inside these ranges and needn't reach their ends.
Inputs may be any that keep to these rules, and one draw needn't show every extreme that they name: `doc_lengths`: each row holds the lengths of 4 documents that fill one sequence of 1024 tokens; its longest document has exactly 512 tokens.
All inputs are finite; a program needn't handle non-finite values.
Results may differ from the reference program's by a relative error of at most 0.0093.
Values may be sent and summed in bfloat16 or wider, within the bound.
No kernel may reach another device: no remote copies, remote signals or barrier semaphores. Data moves between devices by JAX's collectives and lax.ppermute only.
A program may use at most 256 MiB of HBM per device.

```python
import math
import jax
import jax.numpy as jnp
import numpy as np
from jax import lax

D = 1024
HEADS = 16
HD = 64
ROT = 16
FF = 4096
M = 64
LEN = 1024
DOCS = 4
SEQS = 32
TOKENS = 32768


def with_ends(values, own_key, low, top_value):
    index_at = [jax.random.randint(jax.random.fold_in(own_key, axis), (), 0, length) for axis, length in enumerate(values.shape)]
    longest = values.shape.index(max(values.shape))
    next_to = index_at[:longest] + [(index_at[longest] + 1) % values.shape[longest]] + index_at[longest + 1:]
    return values.at[tuple(index_at)].set(low).at[tuple(next_to)].set(top_value)


def with_spikes(drawn, stream_key, source, target, blocks, factor):
    owner, partner = [(jnp.arange(drawn.shape[position]) // (drawn.shape[position] // blocks)).reshape([-1 if axis == position else 1 for axis in range(drawn.ndim)]) for position in (source, target)]
    chosen = jax.random.permutation(stream_key, blocks)[partner]
    strong = (owner == chosen) | (owner == (partner + blocks // 2) % blocks)
    return jnp.where(strong, factor * drawn, drawn)


def levels(own_key, shape, shards, low, top_value):
    loudness = 1.0
    for dim, shards_of in shards:
        heights = jax.random.uniform(jax.random.fold_in(jax.random.fold_in(own_key, 6), dim), (shards_of,), jnp.float32, low / len(shards), top_value / len(shards))
        loudness = loudness * jnp.repeat(jnp.exp(heights), shape[dim] // shards_of).reshape((-1,) + (1,) * (len(shape) - 1 - dim))
    return loudness


def profile(number_of, total, bound, lean):
    loads = [(1 << 20) // math.isqrt(standing ** lean) + 1 for standing in range(2, number_of + 1)]
    spare, counts = total - bound - (number_of - 1), [1] * (number_of - 1)
    while spare > 0:
        candidates = [i for i in range(number_of - 1) if counts[i] < bound]
        whole, budget = sum([loads[i] for i in candidates]), spare
        for i in candidates:
            addition = min(bound - counts[i], max(1, budget * loads[i] // whole), spare)
            counts[i] = counts[i] + addition
            spare = spare - addition
    return np.array([bound] + counts)


def uneven(key, number_of, total, most, slope):
    if number_of == 2:
        one = jax.random.randint(key, (), max(1, total - most), min(most, total - 1) + 1)
        return jnp.stack([one, total - one])
    sizes = jnp.asarray(profile(number_of, total, most, slope), jnp.int32)
    couples = (number_of - 1) // 2
    donor, sink = sizes[1:1 + 2 * couples:2], sizes[2:2 + 2 * couples:2]
    margin = jnp.minimum(donor - 1, most - sink)
    moved = jax.random.randint(jax.random.fold_in(key, 1), (couples,), 0, 1 << 20) % (margin + 1)
    sizes = sizes.at[1:1 + 2 * couples:2].set(donor - moved).at[2:2 + 2 * couples:2].set(sink + moved)
    return sizes[jax.random.permutation(jax.random.fold_in(key, 2), number_of)]


def scatter_about(key, extent, spread, most, cuts=(), kind=jnp.bfloat16):
    values = spread * jax.random.normal(key, extent, jnp.float32)
    if cuts:
        values = values * levels(key, extent, cuts, -0.22, 0.18)
    return jnp.clip(values, -most, most).astype(kind)


def bell_draw_with(own_key, extent, spread, reach, shards, heavy, kind=jnp.bfloat16):
    entries = spread * jax.random.normal(own_key, extent, jnp.float32)
    if shards:
        entries = entries * levels(own_key, extent, shards, -0.22, 0.18)
    return jnp.clip(with_spikes(entries, jax.random.fold_in(own_key, 3), *heavy), -reach, reach).astype(kind)


def setup_inputs(seed: int = 0) -> dict:
    arg_keys = jax.random.split(jax.random.key(seed), 16)
    tokens = bell_draw_with(arg_keys[0], (TOKENS, D), 1.0, 12.0, ((0, 32),), (0, 1, 32, 2.75))
    ln_gain = jnp.clip(1.0 + 0.18 * jax.random.normal(arg_keys[1], (D,), jnp.float32), 0.099609375, 1.8984375).astype(jnp.bfloat16)
    ln_bias = scatter_about(arg_keys[2], (D,), 0.3, 1.75, ((0, 32),))
    qkv_weight = scatter_about(arg_keys[3], (D, 3 * D), D ** -0.5, 0.1875, ((0, 32),))
    qkv_bias = scatter_about(arg_keys[4], (3 * D,), 0.3, 1.75, ((0, 32),))
    out_weight = scatter_about(arg_keys[5], (D, D), (D // 16) ** -0.5, 0.75, ((0, 32),))
    out_bias = scatter_about(arg_keys[6], (D,), 0.3, 1.75, ((0, 32),))
    fc1_weight = scatter_about(arg_keys[7], (D, FF), D ** -0.5, 0.1875, ((0, 32),))
    fc1_bias = scatter_about(arg_keys[8], (FF,), 0.5, 3.0, ((0, 32),))
    fc2_weight = scatter_about(arg_keys[9], (FF, D), FF ** -0.5, 0.09375, ((0, 32),))
    fc2_bias = scatter_about(arg_keys[10], (D,), 0.3, 1.75, ((0, 32),))
    cotangent = scatter_about(arg_keys[11], (TOKENS, D), 1.0, 6.0, ((0, 32),), jnp.float32)
    doc_lengths = jax.vmap(lambda own: uneven(own, DOCS, LEN, LEN // 2, 2))(jax.random.split(arg_keys[12], SEQS)).reshape((SEQS, DOCS)).astype(jnp.int32)
    node_seeds = with_ends(jax.random.randint(arg_keys[13], (M, HD), 0, 1024), jax.random.fold_in(arg_keys[13], 1), 0, 1023).astype(jnp.int32)
    node_weights = with_ends(jax.random.randint(arg_keys[14], (M,), 1, 17), jax.random.fold_in(arg_keys[14], 1), 1, 16).astype(jnp.int32)
    return dict(tokens=tokens, ln_gain=ln_gain, ln_bias=ln_bias, qkv_weight=qkv_weight, qkv_bias=qkv_bias, out_weight=out_weight, out_bias=out_bias, fc1_weight=fc1_weight, fc1_bias=fc1_bias, fc2_weight=fc2_weight, fc2_bias=fc2_bias, cotangent=cotangent, doc_lengths=doc_lengths, node_seeds=node_seeds, node_weights=node_weights)


@jax.custom_vjp
def low(v):
    return lax.optimization_barrier(v.astype(jnp.bfloat16)).astype(jnp.float32)

@jax.custom_vjp
def low_back(v):
    return v

def low_keep(v):
    return (low(v), None)

def low_pass(kept, grad):
    return (grad,)

def back_keep(v):
    return (v, None)

def back_low(kept, grad):
    return (low(grad),)
low.defvjp(low_keep, low_pass)
low_back.defvjp(back_keep, back_low)
feature_scale = 0.2
epsilon = 1e-05
precise = lax.Precision.HIGHEST

def tables(node_seeds, node_weights):
    width = node_seeds.shape[1]
    uniform_pts = (node_seeds.astype(jnp.float32) + 0.5) / 1024.0
    nodes = math.sqrt(2.0) * lax.erf_inv(2.0 * uniform_pts - 1.0)
    order = jnp.arange(width).astype(jnp.float32)
    scales = jnp.where(order[:, None] == 0.0, math.sqrt(1.0 / width), math.sqrt(2.0 / width))
    basis = scales * jnp.cos(math.pi * (2.0 * order[None, :] + 1.0) * order[:, None] / (2.0 * width))
    projection = jnp.dot(nodes, basis, precision=precise)
    weights_float = node_weights.astype(jnp.float32)
    return (projection, weights_float / jnp.sum(weights_float))

def layout(lengths):
    ends = jnp.cumsum(lengths).astype(jnp.int32)
    starts = (ends - lengths).astype(jnp.int32)
    places = jnp.arange(LEN, dtype=jnp.int32)
    doc_ids = lax.optimization_barrier(jnp.sum((places[:, None] >= ends[None, :]).astype(jnp.int32), axis=1)).astype(jnp.int32)
    owners = doc_ids[:, None] == jnp.arange(DOCS, dtype=jnp.int32)[None, :]
    begins = lax.optimization_barrier(jnp.sum(jnp.where(owners, starts[None, :], 0), axis=1)).astype(jnp.int32)
    return (doc_ids, (places - begins).astype(jnp.float32))

def rotary(positions):
    half_rot = ROT // 2
    freqs = 10000.0 ** (-2.0 * jnp.arange(half_rot).astype(jnp.float32) / ROT)
    angles = positions[:, None] * freqs[None, :]
    return (jnp.cos(angles), jnp.sin(angles))

def rotate(heads, cos_table, sin_table):
    half_rot = cos_table.shape[1]
    first = heads[..., :half_rot]
    second = heads[..., half_rot:2 * half_rot]
    rest = heads[..., 2 * half_rot:]
    cos_wide = cos_table[:, None, :]
    sin_wide = sin_table[:, None, :]
    return jnp.concatenate([first * cos_wide - second * sin_wide, second * cos_wide + first * sin_wide, rest], axis=-1)

def features(heads, cos_table, sin_table, projection):
    turned = feature_scale * rotate(heads, cos_table, sin_table)
    exponent = jnp.einsum('lhd,md->lhm', turned, projection, precision=precise)
    exponent = exponent - 0.5 * lax.optimization_barrier(jnp.sum(turned * turned, axis=-1, keepdims=True))
    return jnp.exp(exponent)

def matmul(left, right):
    return jnp.dot(left, right, precision=precise, preferred_element_type=jnp.float32)

def attend(mixed_seq, lengths, projection, quad):
    doc_ids, positions = layout(lengths)
    cos_table, sin_table = rotary(positions)
    query_heads = mixed_seq[:, :D].reshape(LEN, HEADS, HD)
    key_heads = mixed_seq[:, D:2 * D].reshape(LEN, HEADS, HD)
    value_heads = mixed_seq[:, 2 * D:].reshape(LEN, HEADS, HD)
    feat_q = low(features(query_heads, cos_table, sin_table, projection) * quad)
    feat_k = low(features(key_heads, cos_table, sin_table, projection))
    values_low = low(value_heads)
    places = jnp.arange(LEN, dtype=jnp.int32)
    mask = (doc_ids[:, None] == doc_ids[None, :]) & (places[:, None] >= places[None, :])
    raw = jnp.einsum('qhm,khm->hqk', feat_q, feat_k, precision=precise)
    scores = low_back(jnp.where(mask[None], raw, 0.0))
    denom = lax.optimization_barrier(jnp.sum(scores, axis=-1))
    numer = low_back(jnp.einsum('hqk,khd->qhd', low(scores), values_low, precision=precise))
    return (numer / denom.T[:, :, None]).reshape(LEN, D)

def forward(params, rows_x, lengths_group, projection, quad):
    norm_gain, norm_shift, joint_weight, joint_bias, attn_weight, attn_bias, up_weight, up_bias, down_weight, down_bias = params
    center = rows_x - lax.optimization_barrier(jnp.mean(rows_x, axis=-1, keepdims=True))
    normed = center * lax.rsqrt(lax.optimization_barrier(jnp.mean(center * center, axis=-1, keepdims=True)) + epsilon)
    hidden_low = low(normed * norm_gain + norm_shift)
    mixed = low_back(matmul(hidden_low, joint_weight) + joint_bias)
    upper = low_back(matmul(hidden_low, up_weight) + up_bias)
    branch_mlp = low_back(matmul(low(jax.nn.gelu(upper, approximate=False)), down_weight) + down_bias)
    group = lengths_group.shape[0]

    def one_sequence(pair):
        return attend(pair[0], pair[1], projection, quad)
    attn = lax.map(jax.checkpoint(one_sequence), (mixed.reshape(group, LEN, 3 * D), lengths_group))
    branch_attn = low_back(matmul(low(attn.reshape(group * LEN, D)), attn_weight) + attn_bias)
    return rows_x + branch_attn + branch_mlp

def reference(tokens, ln_gain, ln_bias, qkv_weight, qkv_bias, out_weight, out_bias, fc1_weight, fc1_bias, fc2_weight, fc2_bias, cotangent, doc_lengths, node_seeds, node_weights):
    projection, quad = tables(node_seeds, node_weights)
    params = (ln_gain.astype(jnp.float32), ln_bias.astype(jnp.float32), qkv_weight.astype(jnp.float32), qkv_bias.astype(jnp.float32), out_weight.astype(jnp.float32), out_bias.astype(jnp.float32), fc1_weight.astype(jnp.float32), fc1_bias.astype(jnp.float32), fc2_weight.astype(jnp.float32), fc2_bias.astype(jnp.float32))
    group = 4
    groups = SEQS // group
    rows_all = tokens.astype(jnp.float32).reshape(groups, group * LEN, D)
    grads_all = cotangent.astype(jnp.float32).reshape(groups, group * LEN, D)
    lengths_all = doc_lengths.reshape(groups, group, DOCS)

    def step(totals, item):
        rows_x, grad_rows, lengths_group = item

        def local(param_set, inputs):
            return forward(param_set, inputs, lengths_group, projection, quad)
        result, pull = jax.vjp(local, params, rows_x)
        param_grads, input_grads = pull(grad_rows)
        totals = jax.tree.map(jnp.add, totals, param_grads)
        return (totals, (result, input_grads))
    zeros = jax.tree.map(jnp.zeros_like, params)
    totals, (results, input_grads) = lax.scan(step, zeros, (rows_all, grads_all, lengths_all))
    return (results.reshape(TOKENS, D), input_grads.reshape(TOKENS, D), totals[0], totals[1], totals[2], totals[3], totals[4], totals[5], totals[6], totals[7], totals[8], totals[9])
```

```python
import functools
import math

import jax
import jax.numpy as jnp
from jax import lax
from jax.experimental import pallas as pl
from jax.experimental.pallas import tpu as pltpu
from jax.sharding import PartitionSpec as P

D = 1024
HEADS = 16
HD = 64
ROT = 16
LEN = 1024
DOCS = 4
FF = 4096
AXES = ("dp", "fsdp")

feature_scale = 0.2
epsilon = 1e-05
precise = lax.Precision.HIGHEST
bf16 = jnp.bfloat16
f32 = jnp.float32


class Grid:
    def __init__(self, dp, fsdp):
        self.dp, self.fsdp = dp, fsdp
        rest = fsdp // 2
        self.nx = 4 if rest % 16 == 0 else 2
        self.nz = rest // self.nx
        self.ny = dp
        self.n = dp * fsdp
        self.sizes = {"y": self.ny, "z": self.nz, "x": self.nx, "c": 2}
        self.stride = {"y": fsdp, "z": self.nx * 2, "x": 2, "c": 1}

    def digits(self):
        y = lax.axis_index("dp")
        f = lax.axis_index("fsdp")
        return {"y": y, "z": f // (self.nx * 2), "x": (f // 2) % self.nx, "c": f % 2}

    def swap(self, value, digit, k):
        stride = self.stride[digit]
        size = self.sizes[digit]
        pairs = []
        for i in range(self.n):
            d = (i // stride) % size
            pairs.append((i, i + ((d ^ k) - d) * stride))
        return lax.ppermute(value, AXES, pairs)


def place(pieces, outs, moves):
    n_in = len(pieces)
    n_out = len(outs)

    def body(*refs):
        ins, res, sem = refs[:n_in], refs[n_in : n_in + n_out], refs[-1]
        copies = []
        for i, (src, src_at, dst, dst_at) in enumerate(moves):
            copies.append(
                pltpu.make_async_copy(ins[src].at[src_at()], res[dst].at[dst_at()], sem.at[i])
            )
        for copy in copies:
            copy.start()
        for copy in copies:
            copy.wait()

    total = sum(math.prod(o.shape) * o.dtype.itemsize for o in outs)
    return pl.pallas_call(
        body,
        out_shape=tuple(outs),
        in_specs=[pl.BlockSpec(memory_space=pl.ANY)] * n_in,
        out_specs=tuple([pl.BlockSpec(memory_space=pl.ANY)] * n_out),
        scratch_shapes=[pltpu.SemaphoreType.DMA((len(moves),))],
        cost_estimate=pl.CostEstimate(flops=0, transcendentals=0, bytes_accessed=2 * total),
        name="place",
    )(*pieces)


def gather(grid, shard, cut, fields):
    rows, cols = shard.shape
    ny, nz, nx = grid.ny, grid.nz, grid.nx
    dt = shard.dtype
    spans = ((0, cut), (cut, cols))

    pieces = [shard] + [grid.swap(shard, "z", k) for k in range(1, nz)]
    outs = [jax.ShapeDtypeStruct((nz, rows, hi - lo), dt) for lo, hi in spans]
    moves = []
    for k in range(nz):
        for half, (lo, hi) in enumerate(spans):
            moves.append(
                (
                    k,
                    lambda lo=lo, hi=hi: (slice(None), pl.ds(lo, hi - lo)),
                    half,
                    lambda k=k: (grid.digits()["z"] ^ k,),
                )
            )
    part_a, part_b = place(pieces, outs, moves)

    pieces_a = [part_a] + [grid.swap(part_a, "x", k) for k in range(1, nx)]
    pieces_b = [part_b] + [grid.swap(part_b, "y", k) for k in range(1, ny)]
    (part_a,) = place(
        pieces_a,
        [jax.ShapeDtypeStruct((nz, nx) + part_a.shape[1:], dt)],
        [
            (k, lambda: (slice(None),), 0, lambda k=k: (slice(None), grid.digits()["x"] ^ k))
            for k in range(nx)
        ],
    )
    (part_b,) = place(
        pieces_b,
        [jax.ShapeDtypeStruct((ny, nz) + part_b.shape[1:], dt)],
        [(k, lambda: (slice(None),), 0, lambda k=k: (grid.digits()["y"] ^ k,)) for k in range(ny)],
    )
    pieces_a = [part_a] + [grid.swap(part_a, "y", k) for k in range(1, ny)]
    pieces_b = [part_b] + [grid.swap(part_b, "x", k) for k in range(1, nx)]
    every = []
    for half, group in ((0, pieces_a), (1, pieces_b)):
        for k, piece in enumerate(group):
            every.append((half, k, 0, piece))
            every.append((half, k, 1, grid.swap(piece, "c", 1)))
    outs = [
        jax.ShapeDtypeStruct((ny, nz, nx, 2, blocks, rows, width // blocks), dt)
        for _, width, blocks in fields
    ]
    moves = []
    for p, (half, k, core, _) in enumerate(every):
        lo, hi = spans[half]
        for o, (first, width, blocks) in enumerate(fields):
            step = width // blocks
            for b in range(blocks):
                start, end = max(lo, first + b * step), min(hi, first + (b + 1) * step)
                if start >= end:
                    continue

                def src_at(start=start, end=end, lo=lo):
                    return (slice(None), slice(None), slice(None), pl.ds(start - lo, end - start))

                def dst_at(half=half, k=k, core=core, b=b, start=start, end=end, at=first + b * step):
                    d = grid.digits()
                    tail = (d["c"] ^ core, b, slice(None), pl.ds(start - at, end - start))
                    if half == 0:
                        return (d["y"] ^ k, slice(None), slice(None)) + tail
                    return (slice(None), slice(None), d["x"] ^ k) + tail

                moves.append((p, src_at, o, dst_at))
    full = place([e[3] for e in every], outs, moves)
    return [
        w.reshape(grid.n * blocks * rows, width // blocks)
        for w, (_, width, blocks) in zip(full, fields)
    ]


def pick(value, axis, index):
    return lax.dynamic_index_in_dim(value, index, axis, keepdims=False)


def reduce_to_owner(grid, grad):
    n = grid.n
    rows = grad.shape[0] // n
    cols = grad.shape[1]
    d = grid.digits()
    ny, nz, nx = grid.ny, grid.nz, grid.nx
    whole = grad.reshape(ny, nz, nx, 2, rows, cols)
    got = grid.swap(pick(whole, 3, 1 - d["c"]), "c", 1)
    terms = [pick(whole, 3, d["c"]), got]

    def total(parts):
        out = parts[0].astype(f32)
        for part in parts[1:]:
            out = out + part.astype(f32)
        return out

    halves = []
    for half in range(2):
        lo = half * (cols // 2)
        now = [t[..., lo : lo + cols // 2] for t in terms]
        order = (("x", 2), ("y", 0)) if half == 0 else (("y", 0), ("x", 1))
        for digit, axis in order:
            size = grid.sizes[digit]
            arrived = [
                grid.swap(total([pick(t, axis, d[digit] ^ k) for t in now]).astype(bf16), digit, k)
                for k in range(1, size)
            ]
            now = [pick(t, axis, d[digit]) for t in now] + arrived
        halves.append(total(now).astype(bf16))
    joint = jnp.concatenate(halves, axis=-1)
    arrived = [grid.swap(pick(joint, 0, d["z"] ^ k), "z", k) for k in range(1, nz)]
    return total([pick(joint, 0, d["z"])] + arrived)


def reduce_small(grid, grad):
    d = grid.digits()
    now = grad.reshape(grid.ny, grid.nz, grid.nx, 2, grad.shape[1])
    for digit, axis in (("c", 3), ("x", 2), ("y", 0), ("z", 0)):
        mine = pick(now, axis, d[digit])
        for k in range(1, grid.sizes[digit]):
            mine = mine + grid.swap(pick(now, axis, d[digit] ^ k), digit, k)
        now = mine
    return now


def tables(node_seeds, node_weights):
    width = node_seeds.shape[1]
    uniform_pts = (node_seeds.astype(jnp.float32) + 0.5) / 1024.0
    nodes = math.sqrt(2.0) * lax.erf_inv(2.0 * uniform_pts - 1.0)
    order = jnp.arange(width).astype(jnp.float32)
    scales = jnp.where(order[:, None] == 0.0, math.sqrt(1.0 / width), math.sqrt(2.0 / width))
    basis = scales * jnp.cos(
        math.pi * (2.0 * order[None, :] + 1.0) * order[:, None] / (2.0 * width)
    )
    projection = jnp.dot(nodes, basis, precision=precise)
    weights_float = node_weights.astype(jnp.float32)
    return (projection, weights_float / jnp.sum(weights_float))


def layout(lengths):
    ends = jnp.cumsum(lengths)
    starts = ends - lengths
    places = jnp.arange(LEN, dtype=jnp.int32)
    doc_ids = jnp.sum((places[:, None] >= ends[None, :]).astype(jnp.int32), axis=1)
    owners = doc_ids[:, None] == jnp.arange(DOCS, dtype=jnp.int32)[None, :]
    begins = jnp.sum(jnp.where(owners, starts[None, :], 0), axis=1)
    return (doc_ids, (places - begins).astype(jnp.float32))


def rotary(positions):
    half_rot = ROT // 2
    freqs = 10000.0 ** (-2.0 * jnp.arange(half_rot).astype(jnp.float32) / ROT)
    angles = positions[:, None] * freqs[None, :]
    return (jnp.cos(angles), jnp.sin(angles))


def rotate(heads, cos_table, sin_table):
    half_rot = cos_table.shape[1]
    first = heads[..., :half_rot]
    second = heads[..., half_rot : 2 * half_rot]
    rest = heads[..., 2 * half_rot :]
    cos_wide = cos_table[:, None, :]
    sin_wide = sin_table[:, None, :]
    return jnp.concatenate(
        [first * cos_wide - second * sin_wide, second * cos_wide + first * sin_wide, rest], axis=-1
    )


def features(heads, cos_table, sin_table, projection):
    turned = feature_scale * rotate(heads, cos_table, sin_table)
    exponent = jnp.einsum("lhd,md->lhm", turned, projection, precision=precise)
    exponent = exponent - 0.5 * jnp.sum(turned * turned, axis=-1, keepdims=True)
    return jnp.exp(exponent)


def plain_dot(left, right):
    return jnp.dot(left, right, preferred_element_type=jnp.float32)


def outer_sum(left, right, out=jnp.float32):
    return lax.dot_general(left, right, (((0,), (0,)), ((), ())), preferred_element_type=out)


def back_proj(left, right):
    return lax.dot_general(
        left, right, (((1,), (1,)), ((), ())), preferred_element_type=jnp.float32
    )


def gelu_slope(upper):
    return 0.5 * (1.0 + lax.erf(upper / math.sqrt(2.0))) + upper * jnp.exp(
        -0.5 * upper * upper
    ) / math.sqrt(2.0 * math.pi)


def block_mask(doc_ids, first, block):
    places = jnp.arange(doc_ids.shape[0], dtype=jnp.int32)
    rows_here = places[first : first + block]
    same_doc = doc_ids[first : first + block, None] == doc_ids[None, :]
    return same_doc & (rows_here[:, None] >= places[None, :])


def attend(fq_low, fk_low, values_low, doc_ids):
    seq_len = doc_ids.shape[0]
    block = min(512, seq_len)
    outputs = []
    denoms = []
    for first in range(0, seq_len, block):
        mask = block_mask(doc_ids, first, block)
        raw = jnp.einsum(
            "qhm,khm->hqk",
            fq_low[first : first + block],
            fk_low,
            preferred_element_type=jnp.float32,
        )
        scores = jnp.where(mask[None], raw, 0.0)
        denom = jnp.sum(scores, axis=-1)
        numer = jnp.einsum(
            "hqk,khd->qhd",
            scores.astype(jnp.bfloat16),
            values_low,
            preferred_element_type=jnp.float32,
        )
        outputs.append(numer / denom.T[:, :, None])
        denoms.append(denom)
    return (jnp.concatenate(outputs, axis=0), jnp.concatenate(denoms, axis=1))


def attend_back(fq_low, fk_low, values_low, doc_ids, grad_out, attn_out, denom):
    seq_len = doc_ids.shape[0]
    block = min(512, seq_len)
    d_values = jnp.zeros(values_low.shape, jnp.float32)
    d_fk = jnp.zeros(fk_low.shape, jnp.float32)
    d_fq_parts = []
    for first in range(0, seq_len, block):
        mask = block_mask(doc_ids, first, block)
        fq_block = fq_low[first : first + block]
        raw = jnp.einsum("qhm,khm->hqk", fq_block, fk_low, preferred_element_type=jnp.float32)
        scores_low = jnp.where(mask[None], raw, 0.0).astype(jnp.bfloat16)
        den_block = denom[:, first : first + block].T
        grad_block = grad_out[first : first + block]
        d_num_low = (grad_block / den_block[:, :, None]).astype(jnp.bfloat16)
        d_denom = -jnp.sum(grad_block * attn_out[first : first + block], axis=-1) / den_block
        d_prod = jnp.einsum(
            "qhd,khd->hqk", d_num_low, values_low, preferred_element_type=jnp.float32
        )
        d_scores_low = jnp.where(
            mask[None],
            (d_prod + d_denom.T[:, :, None]).astype(jnp.bfloat16),
            jnp.zeros((), jnp.bfloat16),
        )
        d_values = d_values + jnp.einsum(
            "hqk,qhd->khd", scores_low, d_num_low, preferred_element_type=jnp.float32
        )
        d_fq_parts.append(
            jnp.einsum("hqk,khm->qhm", d_scores_low, fk_low, preferred_element_type=jnp.float32)
        )
        d_fk = d_fk + jnp.einsum(
            "hqk,qhm->khm", d_scores_low, fq_block, preferred_element_type=jnp.float32
        )
    return (jnp.concatenate(d_fq_parts, axis=0), d_fk, d_values)


def shards(
    grid,
    tokens,
    ln_gain,
    ln_bias,
    qkv_weight,
    qkv_bias,
    out_weight,
    out_bias,
    fc1_weight,
    fc1_bias,
    fc2_weight,
    fc2_bias,
    cotangent,
    doc_lengths,
    node_seeds,
    node_weights,
):
    n = grid.n
    rows = qkv_weight.shape[0]
    staged = rows % 16 == 0
    vectors = (ln_gain, ln_bias, qkv_bias, out_bias, fc1_bias, fc2_bias)
    small = jnp.concatenate(vectors)
    per_row = small.shape[0] // rows
    small = jnp.pad(small.reshape(rows, per_row), ((0, 0), (0, 128 - per_row)))
    if staged:
        first = jnp.concatenate([qkv_weight, small], axis=1)
        joint_weight, small_all = gather(grid, first, 13 * 128, ((0, 3072, 1), (3072, 128, 1)))
        blocks = fc2_weight.shape[0] // rows
        folded = fc2_weight.reshape(blocks, rows, D).transpose(1, 0, 2).reshape(rows, blocks * D)
        second = jnp.concatenate([out_weight, fc1_weight, folded], axis=1)
        attn_weight, up_weight, down_weight = gather(
            grid, second, 9 * 512, ((0, D, 1), (D, FF, 1), (D + FF, FF, blocks))
        )
    else:
        joint_weight, small_all, attn_weight, up_weight, down_weight = [
            lax.all_gather(w, AXES, axis=0, tiled=True)
            for w in (qkv_weight, small, out_weight, fc1_weight, fc2_weight)
        ]
    small_all = small_all[:, :per_row].reshape(n, rows * per_row)
    wide = []
    at = 0
    for v in vectors:
        wide.append(small_all[:, at : at + v.shape[0]].reshape(n * v.shape[0]).astype(f32))
        at += v.shape[0]
    norm_gain, norm_shift, joint_bias, attn_bias, up_bias, down_bias = wide

    rows_x = tokens.astype(jnp.float32)
    center = rows_x - jnp.mean(rows_x, axis=-1, keepdims=True)
    inv_std = lax.rsqrt(jnp.mean(center * center, axis=-1, keepdims=True) + epsilon)
    normed = center * inv_std
    hidden = normed * norm_gain + norm_shift
    hidden_low = hidden.astype(jnp.bfloat16)
    dy_low = cotangent.astype(jnp.bfloat16)
    dy_sums = jnp.sum(dy_low.astype(jnp.float32), axis=0)

    mixed = plain_dot(hidden_low, joint_weight) + joint_bias
    projection, quad = tables(node_seeds, node_weights)
    doc_ids, positions = layout(doc_lengths[0])
    cos_table, sin_table = rotary(positions)
    query_heads = mixed[:, :D].reshape(LEN, HEADS, HD)
    key_heads = mixed[:, D : 2 * D].reshape(LEN, HEADS, HD)
    values_low = mixed[:, 2 * D :].reshape(LEN, HEADS, HD).astype(jnp.bfloat16)
    fq_low = (features(query_heads, cos_table, sin_table, projection) * quad).astype(jnp.bfloat16)
    fk_low = features(key_heads, cos_table, sin_table, projection).astype(jnp.bfloat16)
    attn_seq, denom = attend(fq_low, fk_low, values_low, doc_ids)
    attn_low = attn_seq.reshape(LEN, D).astype(jnp.bfloat16)

    branch_attn = plain_dot(attn_low, attn_weight) + attn_bias
    g_attn_weight = outer_sum(attn_low, dy_low, bf16)
    grad_out = back_proj(dy_low, attn_weight).reshape(LEN, HEADS, HD)
    d_fq, d_fk, d_values = attend_back(
        fq_low, fk_low, values_low, doc_ids, grad_out, attn_seq, denom
    )

    def feature_pair(query_part, key_part):
        return (
            features(query_part, cos_table, sin_table, projection) * quad,
            features(key_part, cos_table, sin_table, projection),
        )

    unused, pull = jax.vjp(feature_pair, query_heads, key_heads)
    d_queries, d_keys = pull((d_fq, d_fk))
    d_mixed_low = jnp.concatenate(
        [d_queries.reshape(LEN, D), d_keys.reshape(LEN, D), d_values.reshape(LEN, D)], axis=1
    ).astype(jnp.bfloat16)
    g_joint_weight = outer_sum(hidden_low, d_mixed_low, bf16)
    g_joint_bias = jnp.sum(d_mixed_low.astype(jnp.float32), axis=0)

    upper = plain_dot(hidden_low, up_weight) + up_bias
    act_low = jax.nn.gelu(upper, approximate=False).astype(jnp.bfloat16)
    g_down_weight = outer_sum(act_low, dy_low, bf16)
    d_up_low = (back_proj(dy_low, down_weight) * gelu_slope(upper)).astype(jnp.bfloat16)
    g_up_weight = outer_sum(hidden_low, d_up_low, bf16)
    g_up_bias = jnp.sum(d_up_low.astype(jnp.float32), axis=0)
    branch_mlp = plain_dot(act_low, down_weight) + down_bias
    output = rows_x + branch_attn + branch_mlp

    d_hidden = back_proj(d_mixed_low, joint_weight) + back_proj(d_up_low, up_weight)
    g_norm_gain = jnp.sum(d_hidden * normed, axis=0)
    g_norm_shift = jnp.sum(d_hidden, axis=0)
    d_normed = d_hidden * norm_gain
    mean_grad = jnp.mean(d_normed, axis=-1, keepdims=True)
    mean_cross = jnp.mean(d_normed * normed, axis=-1, keepdims=True)
    input_grad = cotangent + inv_std * (d_normed - mean_grad - normed * mean_cross)

    grads = (g_norm_gain, g_norm_shift, g_joint_bias, dy_sums, g_up_bias)
    packed = jnp.concatenate([g.reshape(n, -1) for g in grads], axis=1)
    if staged:
        attn_part = reduce_to_owner(grid, jnp.concatenate([g_attn_weight, g_joint_weight], axis=1))
        s_attn, s_joint = attn_part[:, :D], attn_part[:, D:]
        s_down = reduce_to_owner(grid, g_down_weight)
        s_up = reduce_to_owner(grid, g_up_weight)
        s_small = reduce_small(grid, packed)
    else:
        s_attn, s_joint, s_down, s_up = [
            lax.psum_scatter(g.astype(f32), AXES, scatter_dimension=0, tiled=True)
            for g in (g_attn_weight, g_joint_weight, g_down_weight, g_up_weight)
        ]
        s_small = lax.psum_scatter(packed, AXES, scatter_dimension=0, tiled=True)[0]
    small_outs = []
    at = 0
    for g in grads:
        small_outs.append(s_small[at : at + g.shape[0] // n])
        at += g.shape[0] // n
    s_gain, s_shift, s_joint_bias, s_dy, s_up_bias = small_outs
    return (
        output,
        input_grad,
        s_gain,
        s_shift,
        s_joint,
        s_joint_bias,
        s_attn,
        s_dy,
        s_up,
        s_up_bias,
        s_down,
        s_dy,
    )


def solution(mesh):
    grid = Grid(mesh.shape["dp"], mesh.shape["fsdp"])
    rows2, rows1 = P(AXES, None), P(AXES)
    in_specs = (
        rows2,
        rows1,
        rows1,
        rows2,
        rows1,
        rows2,
        rows1,
        rows2,
        rows1,
        rows2,
        rows1,
        rows2,
        rows2,
        P(),
        P(),
    )
    out_specs = (
        rows2,
        rows2,
        rows1,
        rows1,
        rows2,
        rows1,
        rows2,
        rows1,
        rows2,
        rows1,
        rows2,
        rows1,
    )
    return jax.shard_map(
        functools.partial(shards, grid),
        mesh=mesh,
        in_specs=in_specs,
        out_specs=out_specs,
        check_vma=False,
    )
```

```python
import functools
import math

import jax
import jax.numpy as jnp
from jax import lax
from jax.experimental import pallas as pl
from jax.experimental.pallas import tpu as pltpu
from jax.sharding import PartitionSpec as P

D = 1024
HEADS = 16
HD = 64
ROT = 16
LEN = 1024
DOCS = 4
FF = 4096
AXES = ("dp", "fsdp")
PARTS = 2
BLOCK = 512

feature_scale = 0.2
epsilon = 1e-05
precise = lax.Precision.HIGHEST
bf16 = jnp.bfloat16
f32 = jnp.float32


class Grid:
    def __init__(self, dp, fsdp):
        self.dp, self.fsdp = dp, fsdp
        rest = fsdp // 2
        self.nx = 4 if rest % 16 == 0 else 2
        self.nz = rest // self.nx
        self.ny = dp
        self.n = dp * fsdp
        self.sizes = {"y": self.ny, "z": self.nz, "x": self.nx, "c": 2}
        self.stride = {"y": fsdp, "z": self.nx * 2, "x": 2, "c": 1}

    def digits(self):
        y = lax.axis_index("dp")
        f = lax.axis_index("fsdp")
        return {"y": y, "z": f // (self.nx * 2), "x": (f // 2) % self.nx, "c": f % 2}

    def swap(self, value, digit, k):
        stride = self.stride[digit]
        size = self.sizes[digit]
        pairs = []
        for i in range(self.n):
            d = (i // stride) % size
            pairs.append((i, i + ((d ^ k) - d) * stride))
        return lax.ppermute(value, AXES, pairs)


def place(pieces, outs, moves):
    n_in = len(pieces)
    n_out = len(outs)

    def body(*refs):
        ins, res = refs[:n_in], refs[n_in : n_in + n_out]
        held, sem, done = refs[n_in + n_out : n_in + 2 * n_out], refs[-2], refs[-1]
        copies = []
        for i, (src, src_at, dst, dst_at) in enumerate(moves):
            copies.append(
                pltpu.make_async_copy(ins[src].at[src_at()], held[dst].at[dst_at()], sem.at[i])
            )
        for copy in copies:
            copy.start()
        back = []
        for o in range(n_out):
            for copy, move in zip(copies, moves):
                if move[2] == o:
                    copy.wait()
            back.append(pltpu.make_async_copy(held[o], res[o], done.at[o]))
            back[-1].start()
        for copy in back:
            copy.wait()

    total = sum(math.prod(o.shape) * o.dtype.itemsize for o in outs)
    return pl.pallas_call(
        body,
        out_shape=tuple(outs),
        in_specs=[pl.BlockSpec(memory_space=pl.ANY)] * n_in,
        out_specs=tuple([pl.BlockSpec(memory_space=pl.ANY)] * n_out),
        scratch_shapes=[pltpu.VMEM(o.shape, o.dtype) for o in outs]
        + [pltpu.SemaphoreType.DMA((len(moves),)), pltpu.SemaphoreType.DMA((n_out,))],
        compiler_params=pltpu.CompilerParams(vmem_limit_bytes=total + (2 << 20)),
        cost_estimate=pl.CostEstimate(flops=0, transcendentals=0, bytes_accessed=2 * total),
        name="place",
    )(*pieces)


def gather(grid, shard, cut, fields):
    rows, cols = shard.shape
    ny, nz, nx = grid.ny, grid.nz, grid.nx
    dt = shard.dtype
    spans = ((0, cut), (cut, cols))

    pieces = [shard] + [grid.swap(shard, "z", k) for k in range(1, nz)]
    outs = [jax.ShapeDtypeStruct((nz, rows, hi - lo), dt) for lo, hi in spans]
    moves = []
    for k in range(nz):
        for half, (lo, hi) in enumerate(spans):
            moves.append(
                (
                    k,
                    lambda lo=lo, hi=hi: (slice(None), pl.ds(lo, hi - lo)),
                    half,
                    lambda k=k: (grid.digits()["z"] ^ k,),
                )
            )
    part_a, part_b = place(pieces, outs, moves)

    pieces_a = [part_a] + [grid.swap(part_a, "x", k) for k in range(1, nx)]
    pieces_b = [part_b] + [grid.swap(part_b, "y", k) for k in range(1, ny)]
    (part_a,) = place(
        pieces_a,
        [jax.ShapeDtypeStruct((nz, nx) + part_a.shape[1:], dt)],
        [
            (k, lambda: (slice(None),), 0, lambda k=k: (slice(None), grid.digits()["x"] ^ k))
            for k in range(nx)
        ],
    )
    (part_b,) = place(
        pieces_b,
        [jax.ShapeDtypeStruct((ny, nz) + part_b.shape[1:], dt)],
        [(k, lambda: (slice(None),), 0, lambda k=k: (grid.digits()["y"] ^ k,)) for k in range(ny)],
    )
    pieces_a = [part_a] + [grid.swap(part_a, "y", k) for k in range(1, ny)]
    pieces_b = [part_b] + [grid.swap(part_b, "x", k) for k in range(1, nx)]
    every = []
    for half, group in ((0, pieces_a), (1, pieces_b)):
        for k, piece in enumerate(group):
            every.append((half, k, 0, piece))
            every.append((half, k, 1, grid.swap(piece, "c", 1)))
    outs = [
        jax.ShapeDtypeStruct((ny, nz, nx, 2, blocks, rows, width // blocks), dt)
        for _, width, blocks in fields
    ]
    moves = []
    for p, (half, k, core, _) in enumerate(every):
        lo, hi = spans[half]
        for o, (first, width, blocks) in enumerate(fields):
            step = width // blocks
            for b in range(blocks):
                start, end = max(lo, first + b * step), min(hi, first + (b + 1) * step)
                if start >= end:
                    continue

                def src_at(start=start, end=end, lo=lo):
                    return (slice(None), slice(None), slice(None), pl.ds(start - lo, end - start))

                def dst_at(half=half, k=k, core=core, b=b, start=start, end=end, at=first + b * step):
                    d = grid.digits()
                    tail = (d["c"] ^ core, b, slice(None), pl.ds(start - at, end - start))
                    if half == 0:
                        return (d["y"] ^ k, slice(None), slice(None)) + tail
                    return (slice(None), slice(None), d["x"] ^ k) + tail

                moves.append((p, src_at, o, dst_at))
    full = place([e[3] for e in every], outs, moves)
    return [
        w.reshape(grid.n * blocks * rows, width // blocks)
        for w, (_, width, blocks) in zip(full, fields)
    ]


def fold(groups):
    k, _, _, _, rows, cols = groups[0][0][0].shape
    digits = jnp.stack([value for _, value, _ in groups]).astype(jnp.int32)
    args, in_specs, out_specs, shapes = [], [], [], []
    step = cols // 2
    moved = 0
    for i, (terms, _, n) in enumerate(groups):
        _, a, _, b, _, _ = terms[0].shape
        for j in range(n):
            for term in terms:
                args.append(term)
                in_specs.append(
                    pl.BlockSpec(
                        (1, a, 1, b, rows, step),
                        lambda s, t, ref, i=i, j=j: (s, 0, ref[i] ^ j, 0, 0, t),
                    )
                )
            out_specs.append(pl.BlockSpec((1, a, b, rows, step), lambda s, t, ref: (s, 0, 0, 0, t)))
            shapes.append(jax.ShapeDtypeStruct((k, a, b, rows, cols), bf16))
            moved += (len(terms) + 1) * 2 * k * a * b * rows * cols

    def body(ref, *refs):
        at = 0
        out = len(args)
        for terms, _, n in groups:
            for _ in range(n):
                total = refs[at][:, :, 0].astype(f32)
                for more in refs[at + 1 : at + len(terms)]:
                    total = total + more[:, :, 0].astype(f32)
                refs[out][...] = total.astype(bf16)
                at += len(terms)
                out += 1

    outs = pl.pallas_call(
        body,
        grid_spec=pltpu.PrefetchScalarGridSpec(
            num_scalar_prefetch=1, grid=(k, 2), in_specs=in_specs, out_specs=out_specs
        ),
        out_shape=tuple(shapes),
        compiler_params=pltpu.CompilerParams(vmem_limit_bytes=40 << 20),
        cost_estimate=pl.CostEstimate(flops=moved, transcendentals=0, bytes_accessed=moved),
        name="fold",
    )(digits, *args)
    result = []
    at = 0
    for _, _, n in groups:
        result.append(list(outs[at : at + n]))
        at += n
    return result


def reduce_to_owner(grid, keep_a, send_a, keep_b, send_b):
    k, half, cols = keep_a.shape
    ny, nz, nx = grid.ny, grid.nz, grid.nx
    rows = half // (ny * nz * nx)
    d = grid.digits()
    got_a, got_b = grid.swap(send_a, "c", 1), grid.swap(send_b, "c", 1)
    view = lambda a, n, b: lambda v: v.reshape(k, a, n, b, rows, cols)
    by_x, by_y = view(ny * nz, nx, 1), view(1, ny, nz * nx)
    part_a, part_b = fold(
        [
            ([by_x(keep_a), by_x(got_a)], d["x"], nx),
            ([by_y(keep_b), by_y(got_b)], d["y"], ny),
        ]
    )
    terms_a = [part_a[0]] + [grid.swap(part_a[j], "x", j) for j in range(1, nx)]
    terms_b = [part_b[0]] + [grid.swap(part_b[j], "y", j) for j in range(1, ny)]
    by_y, by_x = view(1, ny, nz), view(nz, nx, 1)
    part_a, part_b = fold(
        [
            ([by_y(v) for v in terms_a], d["y"], ny),
            ([by_x(v) for v in terms_b], d["x"], nx),
        ]
    )
    terms_a = [part_a[0]] + [grid.swap(part_a[j], "y", j) for j in range(1, ny)]
    terms_b = [part_b[0]] + [grid.swap(part_b[j], "x", j) for j in range(1, nx)]
    by_z = view(1, nz, 1)
    part_a, part_b = fold(
        [([by_z(v) for v in terms_a], d["z"], nz), ([by_z(v) for v in terms_b], d["z"], nz)]
    )
    result = []
    for part in (part_a, part_b):
        total = part[0].astype(f32)
        for j in range(1, nz):
            total = total + grid.swap(part[j], "z", j).astype(f32)
        result.append(total.reshape(k, rows, cols))
    return result


def reduce_small(grid, grad):
    d = grid.digits()
    now = grad.reshape(grid.ny, grid.nz, grid.nx, 2, grad.shape[1])
    for digit, axis in (("c", 3), ("x", 2), ("y", 0), ("z", 0)):
        mine = pick(now, axis, d[digit])
        for k in range(1, grid.sizes[digit]):
            mine = mine + grid.swap(pick(now, axis, d[digit] ^ k), digit, k)
        now = mine
    return now


def tables(node_seeds, node_weights):
    width = node_seeds.shape[1]
    uniform_pts = (node_seeds.astype(jnp.float32) + 0.5) / 1024.0
    nodes = math.sqrt(2.0) * lax.erf_inv(2.0 * uniform_pts - 1.0)
    order = jnp.arange(width).astype(jnp.float32)
    scales = jnp.where(order[:, None] == 0.0, math.sqrt(1.0 / width), math.sqrt(2.0 / width))
    basis = scales * jnp.cos(
        math.pi * (2.0 * order[None, :] + 1.0) * order[:, None] / (2.0 * width)
    )
    projection = jnp.dot(nodes, basis, precision=precise)
    weights_float = node_weights.astype(jnp.float32)
    return (projection, weights_float / jnp.sum(weights_float))


def layout(lengths):
    ends = jnp.cumsum(lengths)
    starts = ends - lengths
    places = jnp.arange(LEN, dtype=jnp.int32)
    doc_ids = jnp.sum((places[:, None] >= ends[None, :]).astype(jnp.int32), axis=1)
    owners = doc_ids[:, None] == jnp.arange(DOCS, dtype=jnp.int32)[None, :]
    begins = jnp.sum(jnp.where(owners, starts[None, :], 0), axis=1)
    return (doc_ids, (places - begins).astype(jnp.float32))


def rotary(positions):
    half_rot = ROT // 2
    freqs = 10000.0 ** (-2.0 * jnp.arange(half_rot).astype(jnp.float32) / ROT)
    angles = positions[:, None] * freqs[None, :]
    return (jnp.cos(angles), jnp.sin(angles))


TILE = 256
WIDE = 256
PER = WIDE // HD
STEPS = LEN // TILE
PAIRS = [(q, k) for q in range(STEPS) for k in range(max(0, q - 2), q + 1)]


def nn(a, b):
    return lax.dot_general(a, b, (((1,), (0,)), ((), ())), preferred_element_type=f32)


def nt(a, b):
    return lax.dot_general(a, b, (((1,), (1,)), ((), ())), preferred_element_type=f32)


def halves(v):
    high = v.astype(bf16)
    return high, (v - high.astype(f32)).astype(bf16)


def attention_body(
    rows,
    core_ref,
    hid_ref,
    hid_t_ref,
    dy_ref,
    wq_ref,
    wk_ref,
    wv_ref,
    bq_ref,
    bk_ref,
    bv_ref,
    wo_ref,
    cos_ref,
    left_ref,
    right_ref,
    proj_ref,
    proj_low_ref,
    ones_ref,
    quad_ref,
    doc_col_ref,
    doc_row_ref,
    branch_ref,
    dh_ref,
    keep_qk_ref,
    send_qk_ref,
    keep_vo_ref,
    send_vo_ref,
    sums_ref,
    mask,
    scores,
    yq,
    yk,
    fq,
    fk,
    val,
    val_h,
    fq_t,
    dnum,
    dnum_t,
    cross,
    cross_low,
    att_t,
    num,
    den,
    dfq,
    dfk_t,
    dv_t,
    dmq,
    dmk,
    dmv,
    eq,
    ek,
):
    step = pl.program_id(0)
    span = [pl.ds(r * TILE, TILE) for r in range(STEPS)]
    lane = lax.broadcasted_iota(jnp.int32, (TILE, WIDE), 1) // HD
    ones = ones_ref[...]
    proj, proj_low = proj_ref[...], proj_low_ref[...]

    @pl.when(step == 0)
    def _():
        for i, (q, k) in enumerate(PAIRS):
            here = doc_col_ref[span[q], :] == doc_row_ref[:, span[k]]
            if q == k:
                row = lax.broadcasted_iota(jnp.int32, (TILE, TILE), 0)
                col = lax.broadcasted_iota(jnp.int32, (TILE, TILE), 1)
                here = here & (row >= col)
            mask[i] = jnp.where(here, 1.0, 0.0).astype(bf16)

    for r in range(STEPS):
        hid = hid_ref[span[r], :]
        val[span[r], :] = (nn(hid, wv_ref[...]) + bv_ref[...]).astype(bf16)
        for w_ref, b_ref, y_out, f_out, scale in (
            (wq_ref, bq_ref, yq, fq, True),
            (wk_ref, bk_ref, yk, fk, False),
        ):
            raw = nn(hid, w_ref[...]) + b_ref[...]
            y = (
                raw * cos_ref[span[r], :]
                + pltpu.roll(raw, WIDE - 8, 1) * left_ref[span[r], :]
                + pltpu.roll(raw, 8, 1) * right_ref[span[r], :]
            )
            y_high, y_low = halves(y)
            s_high, s_low = halves(y * y)
            power = nt(y_high, proj) + nt(y_low, proj) + nt(y_high, proj_low)
            power = power - 0.5 * (nn(s_high, ones) + nn(s_low, ones))
            feat = jnp.exp(power)
            if scale:
                feat = feat * quad_ref[...]
            y_out[span[r], :] = y
            f_out[span[r], :] = feat.astype(bf16)
            (eq if scale else ek)[span[r], :] = feat
            if scale:
                fq_t[:, span[r]] = feat.T.astype(bf16)

    def forward(h, carry):
        own = lane == h
        for r in range(STEPS):
            val_h[h, span[r], :] = jnp.where(own, val[span[r], :], jnp.ones((), bf16))
        total = None
        for i, (q, k) in enumerate(PAIRS):
            query = jnp.where(own, fq[span[q], :], jnp.zeros((), bf16))
            tile = nt(query, fk[span[k], :]).astype(bf16) * mask[i]
            scores[h * len(PAIRS) + i] = tile
            part = nn(tile, val_h[h, span[k], :])
            total = part if total is None else total + part
            if k == q:
                num[span[q], :] = jnp.where(own, total, num[span[q], :])
                den[span[q], :] = jnp.where(own, pltpu.roll(total, HD, 1), den[span[q], :])
                total = None
        return carry

    lax.fori_loop(0, PER, forward, 0)

    for r in range(STEPS):
        grad = nt(dy_ref[span[r], :], wo_ref[...])
        inv = 1.0 / den[span[r], :]
        att = num[span[r], :] * inv
        att_low = att.astype(bf16)
        more = nn(att_low, wo_ref[...])

        @pl.when(step == 0)
        def _():
            branch_ref[span[r], :] = more

        @pl.when(step > 0)
        def _():
            branch_ref[span[r], :] = branch_ref[span[r], :] + more

        d_num = grad * inv
        dnum[span[r], :] = d_num.astype(bf16)
        dnum_t[:, span[r]] = d_num.T.astype(bf16)
        att_t[:, span[r]] = att.T.astype(bf16)
        high, low = halves(pltpu.roll(-d_num * att, HD, 1))
        cross[span[r], :] = high
        cross_low[span[r], :] = pltpu.roll(low.astype(f32), HD, 1).astype(bf16)

    def backward(h, carry):
        own = lane == h
        after = lane == lax.rem(h + 1, PER)
        later = lane == lax.rem(h + 2, PER)
        mine = pl.ds(pl.multiple_of(h * HD, HD), HD)
        dfk_t[mine, :] = jnp.zeros((HD, LEN), f32)
        dv_t[mine, :] = jnp.zeros((HD, LEN), f32)
        total = None
        for i, (q, k) in enumerate(PAIRS):
            left = jnp.where(
                own,
                dnum[span[q], :],
                jnp.where(
                    after,
                    cross[span[q], :],
                    jnp.where(later, cross_low[span[q], :], jnp.zeros((), bf16)),
                ),
            )
            tile = nt(left, val_h[h, span[k], :]).astype(bf16) * mask[i]
            part = nn(tile, fk[span[k], :])
            total = part if total is None else total + part
            dfk_t[mine, span[k]] += nn(fq_t[mine, span[q]], tile)
            dv_t[mine, span[k]] += nn(dnum_t[mine, span[q]], scores[h * len(PAIRS) + i])
            if k == q:
                dfq[span[q], :] = jnp.where(own, total, dfq[span[q], :])
                total = None
        return carry

    lax.fori_loop(0, PER, backward, 0)

    sums = [jnp.zeros((1, WIDE), f32)] * 3
    for r in range(STEPS):
        grads = []
        for d_feat, feat, y in (
            (dfq[span[r], :], eq, yq),
            (dfk_t[:, span[r]].T, ek, yk),
        ):
            e_high, e_low = halves(d_feat * feat[span[r], :])
            d_y = nn(e_high, proj) + nn(e_low, proj) + nn(e_high, proj_low)
            d_y = d_y - (nn(e_high, ones) + nn(e_low, ones)) * y[span[r], :]
            grads.append(
                d_y * cos_ref[span[r], :]
                - pltpu.roll(d_y, WIDE - 8, 1) * left_ref[span[r], :]
                - pltpu.roll(d_y, 8, 1) * right_ref[span[r], :]
            )
        grads.append(dv_t[:, span[r]].T)
        lows = [g.astype(bf16) for g in grads]
        for i, out in enumerate((dmq, dmk, dmv)):
            out[span[r], :] = lows[i]
            sums[i] = sums[i] + jnp.sum(lows[i].astype(f32), axis=0, keepdims=True)
        more = nt(lows[0], wq_ref[...]) + nt(lows[1], wk_ref[...]) + nt(lows[2], wv_ref[...])

        @pl.when(step == 0)
        def _():
            dh_ref[span[r], :] = more

        @pl.when(step > 0)
        def _():
            dh_ref[span[r], :] = dh_ref[span[r], :] + more

    for i in range(3):
        sums_ref[pl.ds(i, 1), :] = sums[i]

    for r in range(STEPS):
        rows_of = hid_t_ref[span[r], :]
        keep = r < STEPS // 2
        at = pl.ds((r % (STEPS // 2)) * TILE, TILE)
        qk, vo = (keep_qk_ref, keep_vo_ref) if keep else (send_qk_ref, send_vo_ref)
        qk[0, at, :] = nn(rows_of, dmq[...]).astype(bf16)
        qk[1, at, :] = nn(rows_of, dmk[...]).astype(bf16)
        vo[0, at, pl.ds(pl.multiple_of(step * WIDE, WIDE), WIDE)] = nn(rows_of, dmv[...]).astype(bf16)
    first = core_ref[0] == 0
    for p in range(WIDE // (2 * rows)):
        pair = nn(att_t[pl.ds(p * 2 * rows, 2 * rows), :], dy_ref[...]).astype(bf16)
        even, odd = pair[:rows], pair[rows:]
        at = pl.ds(pl.multiple_of(step * (WIDE // 2), WIDE // 2) + p * rows, rows)
        keep_vo_ref[1, at, :] = jnp.where(first, even, odd)
        send_vo_ref[1, at, :] = jnp.where(first, odd, even)


def attention(core, rows, hid, hid_t, dy, wqk, wv, bqkv, wo, cos_t, left_t, right_t, proj, proj_low, ones, quad, doc_col, doc_row):
    groups = wo.shape[0] // WIDE
    whole = lambda shape: pl.BlockSpec(shape, lambda g: (0, 0), pipeline_mode=pl.Buffered(1))
    col = lambda shift: pl.BlockSpec((D, WIDE), lambda g: (0, g + shift * groups))
    bias = lambda shift: pl.BlockSpec((1, WIDE), lambda g: (0, g + shift * groups))
    half = D // 2
    all_three = pl.BlockSpec((2, half, D), lambda g: (0, 0, 0), pipeline_mode=pl.Buffered(1))
    in_specs = [
        pl.BlockSpec(memory_space=pltpu.SMEM),
        whole((LEN, D)),
        whole((D, LEN)),
        whole((LEN, D)),
        col(0),
        col(1),
        col(0),
        bias(0),
        bias(1),
        bias(2),
        pl.BlockSpec((WIDE, D), lambda g: (g, 0)),
        whole((LEN, WIDE)),
        whole((LEN, WIDE)),
        whole((LEN, WIDE)),
        whole((WIDE, WIDE)),
        whole((WIDE, WIDE)),
        whole((WIDE, WIDE)),
        whole((1, WIDE)),
        whole((LEN, 1)),
        whole((1, LEN)),
    ]
    span = groups * WIDE
    shapes = [
        ((LEN, D), f32, whole((LEN, D))),
        ((LEN, D), f32, whole((LEN, D))),
        ((2, half, span), bf16, pl.BlockSpec((2, half, WIDE), lambda g: (0, 0, g))),
        ((2, half, span), bf16, pl.BlockSpec((2, half, WIDE), lambda g: (0, 0, g))),
        ((2, half, D), bf16, all_three),
        ((2, half, D), bf16, all_three),
        ((8, span), f32, pl.BlockSpec((8, WIDE), lambda g: (0, g))),
    ]
    vm = lambda shape, dt: pltpu.VMEM(shape, dt)
    scratch = [
        vm((len(PAIRS), TILE, TILE), bf16),
        vm((PER * len(PAIRS), TILE, TILE), bf16),
        vm((LEN, WIDE), f32),
        vm((LEN, WIDE), f32),
        vm((LEN, WIDE), bf16),
        vm((LEN, WIDE), bf16),
        vm((LEN, WIDE), bf16),
        vm((PER, LEN, WIDE), bf16),
        vm((WIDE, LEN), bf16),
        vm((LEN, WIDE), bf16),
        vm((WIDE, LEN), bf16),
        vm((LEN, WIDE), bf16),
        vm((LEN, WIDE), bf16),
        vm((WIDE, LEN), bf16),
        vm((LEN, WIDE), f32),
        vm((LEN, WIDE), f32),
        vm((LEN, WIDE), f32),
        vm((WIDE, LEN), f32),
        vm((WIDE, LEN), f32),
        vm((LEN, WIDE), bf16),
        vm((LEN, WIDE), bf16),
        vm((LEN, WIDE), bf16),
        vm((LEN, WIDE), f32),
        vm((LEN, WIDE), f32),
    ]
    return pl.pallas_call(
        functools.partial(attention_body, rows),
        grid=(groups,),
        out_shape=tuple(jax.ShapeDtypeStruct(s, t) for s, t, _ in shapes),
        in_specs=in_specs,
        out_specs=tuple(spec for _, _, spec in shapes),
        scratch_shapes=scratch,
        compiler_params=pltpu.CompilerParams(vmem_limit_bytes=56 << 20),
        cost_estimate=pl.CostEstimate(
            flops=groups * 20 * (1 << 30), transcendentals=0, bytes_accessed=30 << 20
        ),
        name="attention",
    )(core, hid, hid_t, dy, wqk, wqk, wv, bqkv, bqkv, bqkv, wo, cos_t, left_t, right_t, proj, proj_low, ones, quad, doc_col, doc_row)


def mlp_body(
    rows,
    wide,
    core_ref,
    hid_ref,
    hid_t_ref,
    dy_ref,
    w1_ref,
    b1_ref,
    w2_ref,
    out_ref,
    dh_ref,
    keep_1_ref,
    send_1_ref,
    keep_2_ref,
    send_2_ref,
    sums_ref,
    act_t,
    dup,
):
    step = pl.program_id(0)
    block = w2_ref.shape[0]
    tile = 256
    total = jnp.zeros((1, block), f32)
    for r in range(LEN // tile):
        at = pl.ds(r * tile, tile)
        upper = nn(hid_ref[at, :], w1_ref[...]) + b1_ref[...]
        bell = jnp.exp(-0.5 * upper * upper)
        phi = 0.5 + 0.5 * lax.erf(upper * (1.0 / math.sqrt(2.0)))
        act = upper * phi
        act_low = act.astype(bf16)
        act_t[:, at] = act.T.astype(bf16)
        slope = phi + upper * bell * (1.0 / math.sqrt(2.0 * math.pi))
        d_up = (nt(dy_ref[at, :], w2_ref[...]) * slope).astype(bf16)
        dup[at, :] = d_up
        total = total + jnp.sum(d_up.astype(f32), axis=0, keepdims=True)
        more = nn(act_low, w2_ref[...])
        back = nt(d_up, w1_ref[...])

        @pl.when(step == 0)
        def _():
            out_ref[at, :] = more
            dh_ref[at, :] = back

        @pl.when(step > 0)
        def _():
            out_ref[at, :] = out_ref[at, :] + more
            dh_ref[at, :] = dh_ref[at, :] + back

    sums_ref[...] = total
    for r in range(D // tile):
        res = nn(hid_t_ref[pl.ds(r * tile, tile), :], dup[...]).astype(bf16)
        half = D // tile // 2
        out = keep_1_ref if r < half else send_1_ref
        out[0, pl.ds((r % half) * tile, tile), :] = res
    first = core_ref[0] == 0
    for p in range(block // (2 * wide)):
        pair = nn(act_t[pl.ds(p * 2 * wide, 2 * wide), :], dy_ref[...]).astype(bf16)
        for b in range(wide // rows):
            even = pair[b * rows : (b + 1) * rows]
            odd = pair[wide + b * rows : wide + (b + 1) * rows]
            keep_2_ref[b, pl.ds(p * rows, rows), :] = jnp.where(first, even, odd)
            send_2_ref[b, pl.ds(p * rows, rows), :] = jnp.where(first, odd, even)


def mlp(core, rows, wide, block, hid, hid_t, dy, w1, b1, w2):
    units = w2.shape[0]
    grid = units // block
    whole = lambda shape: pl.BlockSpec(shape, lambda g: (0, 0), pipeline_mode=pl.Buffered(1))
    half = D // 2
    pairs = block // (2 * wide)
    folds = wide // rows
    per = D // block
    fold_1 = pl.BlockSpec((1, half, block), lambda g: (g // per, 0, g % per))
    shapes = [
        ((LEN, D), f32, whole((LEN, D))),
        ((LEN, D), f32, whole((LEN, D))),
        ((units // D, half, D), bf16, fold_1),
        ((units // D, half, D), bf16, fold_1),
        ((folds, grid * pairs * rows, D), bf16, pl.BlockSpec((folds, pairs * rows, D), lambda g: (0, g, 0))),
        ((folds, grid * pairs * rows, D), bf16, pl.BlockSpec((folds, pairs * rows, D), lambda g: (0, g, 0))),
        ((1, units), f32, pl.BlockSpec((1, block), lambda g: (0, g))),
    ]
    return pl.pallas_call(
        functools.partial(mlp_body, rows, wide),
        grid=(grid,),
        out_shape=tuple(jax.ShapeDtypeStruct(s, t) for s, t, _ in shapes),
        in_specs=[
            pl.BlockSpec(memory_space=pltpu.SMEM),
            whole((LEN, D)),
            whole((D, LEN)),
            whole((LEN, D)),
            pl.BlockSpec((D, block), lambda g: (0, g)),
            pl.BlockSpec((1, block), lambda g: (0, g)),
            pl.BlockSpec((block, D), lambda g: (g, 0)),
        ],
        out_specs=tuple(spec for _, _, spec in shapes),
        scratch_shapes=[pltpu.VMEM((block, LEN), bf16), pltpu.VMEM((LEN, block), bf16)],
        compiler_params=pltpu.CompilerParams(vmem_limit_bytes=48 << 20),
        cost_estimate=pl.CostEstimate(
            flops=6 * 2 * LEN * D * units, transcendentals=0, bytes_accessed=30 << 20
        ),
        name="mlp",
    )(core, hid, hid_t, dy, w1, b1, w2)


def rest_rows(value, rows, core):
    blocks = value.reshape(-1, 2, rows, value.shape[-1])
    return jnp.concatenate(
        [pick(blocks, 1, core).reshape(-1, value.shape[-1]), pick(blocks, 1, 1 - core).reshape(-1, value.shape[-1])]
    )


def pick(value, axis, index):
    return lax.dynamic_index_in_dim(value, index, axis, keepdims=False)


def alternate(keep, send, rows):
    both = jnp.stack([keep.reshape(-1, rows, keep.shape[-1]), send.reshape(-1, rows, keep.shape[-1])], axis=1)
    return both.reshape(-1, keep.shape[-1])


def shards(
    grid,
    tokens,
    ln_gain,
    ln_bias,
    qkv_weight,
    qkv_bias,
    out_weight,
    out_bias,
    fc1_weight,
    fc1_bias,
    fc2_weight,
    fc2_bias,
    cotangent,
    doc_lengths,
    node_seeds,
    node_weights,
):
    n = grid.n
    rows = qkv_weight.shape[0]
    staged = rows % 32 == 0
    parts = PARTS if staged else 1
    vectors = (ln_gain, ln_bias, qkv_bias, out_bias, fc1_bias, fc2_bias)
    small = jnp.concatenate(vectors)
    per_row = small.shape[0] // rows
    small = jnp.pad(small.reshape(rows, per_row), ((0, 0), (0, 128 - per_row)))
    units = FF // parts
    wide = units // n if staged else 64
    folds = wide // 32
    if staged:
        first = jnp.concatenate(
            [qkv_weight[:, : 2 * D], small, qkv_weight[:, 2 * D :], out_weight], axis=1
        )
        qk_weight, small_all, v_weight, attn_weight = gather(
            grid,
            first,
            2 * D + 128,
            ((0, 2 * D, 1), (2 * D, 128, 1), (2 * D + 128, D, 1), (3 * D + 128, D, 1)),
        )
        up_weights, down_weights = [], []
        split = fc1_weight.reshape(rows, n, parts, wide)
        for m in range(parts):
            folded = fc2_weight[m * wide : (m + 1) * wide].reshape(folds, rows, D)
            packed = jnp.concatenate(
                [split[:, :, m].reshape(rows, units)] + [folded[i] for i in range(folds)], axis=1
            )
            if m == 0:
                packed, qk_weight = lax.optimization_barrier((packed, qk_weight))
            up, down = gather(grid, packed, units, ((0, units, 1), (units, folds * D, folds)))
            up_weights.append(up)
            down_weights.append(down)
    else:
        joint_weight, small_all, attn_weight, up, down = [
            lax.all_gather(w, AXES, axis=0, tiled=True)
            for w in (qkv_weight, small, out_weight, fc1_weight, fc2_weight)
        ]
        qk_weight, v_weight = joint_weight[:, : 2 * D], joint_weight[:, 2 * D :]
        up_weights, down_weights = [up], [down]
    small_all = small_all[:, :per_row].reshape(n, rows * per_row)
    whole = []
    at = 0
    for v in vectors:
        whole.append(small_all[:, at : at + v.shape[0]].reshape(n * v.shape[0]).astype(f32))
        at += v.shape[0]
    norm_gain, norm_shift, joint_bias, attn_bias, up_bias, down_bias = whole

    core = grid.digits()["c"] if staged else jnp.zeros((), jnp.int32)
    core_arg = core.reshape(1).astype(jnp.int32)
    block_rows = rows if staged else 32
    rows_x = tokens.astype(f32)
    center = rows_x - jnp.mean(rows_x, axis=-1, keepdims=True)
    inv_std = lax.rsqrt(jnp.mean(center * center, axis=-1, keepdims=True) + epsilon)
    normed = center * inv_std
    hidden_low = (normed * norm_gain + norm_shift).astype(bf16)
    hidden_t = rest_rows(hidden_low.T, block_rows, core)
    dy_low = cotangent.astype(bf16)
    dy_sums = jnp.sum(dy_low.astype(f32), axis=0)

    projection, quad = tables(node_seeds, node_weights)
    doc_ids, positions = layout(doc_lengths[0])
    cos, sin = rotary(positions)
    flat = jnp.ones((LEN, HD - ROT), f32)
    none = jnp.zeros((LEN, ROT // 2), f32)
    cos_t = feature_scale * jnp.tile(jnp.concatenate([cos, cos, flat], axis=1), (1, PER))
    left_t = feature_scale * jnp.tile(jnp.concatenate([-sin, none, 0 * flat], axis=1), (1, PER))
    right_t = feature_scale * jnp.tile(jnp.concatenate([none, sin, 0 * flat], axis=1), (1, PER))
    eye = jnp.eye(PER, dtype=f32)
    wide_proj = jnp.einsum("ab,jd->ajbd", eye, projection, precision=precise).reshape(WIDE, WIDE)
    near = lax.reduce_precision(wide_proj, 8, 7)
    ones = jnp.kron(eye, jnp.ones((HD, HD), f32)).astype(bf16)

    branch, d_hidden, keep_qk, send_qk, keep_vo, send_vo, joint_sums = attention(
        core_arg,
        block_rows,
        hidden_low,
        hidden_t,
        dy_low,
        qk_weight,
        v_weight,
        joint_bias[None],
        attn_weight,
        cos_t,
        left_t,
        right_t,
        near.astype(bf16),
        (wide_proj - near).astype(bf16),
        ones,
        jnp.tile(quad, PER)[None],
        doc_ids[:, None],
        doc_ids[None],
    )
    split_bias = up_bias.reshape(-1, parts, wide)
    branches, backs, up_sums, mlp_grads = [branch], [d_hidden], [], []
    for m in range(parts):
        more, back, keep_1, send_1, keep_2, send_2, sums = mlp(
            core_arg,
            block_rows,
            wide,
            BLOCK,
            hidden_low,
            hidden_t,
            dy_low,
            up_weights[m],
            split_bias[:, m].reshape(1, units),
            down_weights[m],
        )
        branches.append(more)
        backs.append(back)
        up_sums.append(sums.reshape(-1, 1, wide))
        mlp_grads.append((keep_1, send_1, keep_2, send_2))
    output = rows_x + (attn_bias + down_bias)
    for more in branches:
        output = output + more
    d_hidden = backs[0]
    for back in backs[1:]:
        d_hidden = d_hidden + back

    g_up_bias = jnp.concatenate(up_sums, axis=1).reshape(FF)
    g_joint_bias = joint_sums[:3].reshape(3 * D)
    g_norm_gain = jnp.sum(d_hidden * normed, axis=0)
    g_norm_shift = jnp.sum(d_hidden, axis=0)
    d_normed = d_hidden * norm_gain
    mean_grad = jnp.mean(d_normed, axis=-1, keepdims=True)
    mean_cross = jnp.mean(d_normed * normed, axis=-1, keepdims=True)
    input_grad = cotangent + inv_std * (d_normed - mean_grad - normed * mean_cross)

    grads = (g_norm_gain, g_norm_shift, g_joint_bias, dy_sums, g_up_bias)
    packed = jnp.concatenate([g.reshape(n, -1) for g in grads], axis=1)
    if staged:
        s_qk, s_vo = reduce_to_owner(grid, keep_qk, send_qk, keep_vo, send_vo)
        s_joint = jnp.concatenate([s_qk[0], s_qk[1], s_vo[0]], axis=1)
        s_attn = s_vo[1]
        ups, downs = [], []
        for mine in mlp_grads:
            s_1, s_2 = reduce_to_owner(grid, *mine)
            ups.append(s_1.transpose(1, 0, 2).reshape(rows, n, 1, wide))
            downs.append(s_2.reshape(wide, D))
        s_up = jnp.concatenate(ups, axis=2).reshape(rows, FF)
        s_down = jnp.concatenate(downs, axis=0)
        s_small = reduce_small(grid, packed)
    else:
        flat_of = lambda v: v.transpose(1, 0, 2).reshape(v.shape[1], -1)
        keep_1, send_1, keep_2, send_2 = mlp_grads[0]
        both = (
            alternate(
                jnp.concatenate([flat_of(keep_qk), keep_vo[0]], axis=1),
                jnp.concatenate([flat_of(send_qk), send_vo[0]], axis=1),
                block_rows,
            ),
            alternate(keep_vo[1], send_vo[1], block_rows),
            alternate(flat_of(keep_1), flat_of(send_1), block_rows),
            alternate(*(v.reshape(folds, -1, 32, D).transpose(1, 0, 2, 3).reshape(-1, D) for v in (keep_2, send_2)), wide),
        )
        s_joint, s_attn, s_up, s_down = [
            lax.psum_scatter(g.astype(f32), AXES, scatter_dimension=0, tiled=True) for g in both
        ]
        s_small = lax.psum_scatter(packed, AXES, scatter_dimension=0, tiled=True)[0]
    small_outs = []
    at = 0
    for g in grads:
        small_outs.append(s_small[at : at + g.shape[0] // n])
        at += g.shape[0] // n
    s_gain, s_shift, s_joint_bias, s_dy, s_up_bias = small_outs
    return (
        output,
        input_grad,
        s_gain,
        s_shift,
        s_joint,
        s_joint_bias,
        s_attn,
        s_dy,
        s_up,
        s_up_bias,
        s_down,
        s_dy,
    )


def solution(mesh):
    grid = Grid(mesh.shape["dp"], mesh.shape["fsdp"])
    rows2, rows1 = P(AXES, None), P(AXES)
    in_specs = (
        rows2,
        rows1,
        rows1,
        rows2,
        rows1,
        rows2,
        rows1,
        rows2,
        rows1,
        rows2,
        rows1,
        rows2,
        rows2,
        P(),
        P(),
    )
    out_specs = (
        rows2,
        rows2,
        rows1,
        rows1,
        rows2,
        rows1,
        rows2,
        rows1,
        rows2,
        rows1,
        rows2,
        rows1,
    )
    return jax.shard_map(
        functools.partial(shards, grid),
        mesh=mesh,
        in_specs=in_specs,
        out_specs=out_specs,
        check_vma=False,
    )
```

```python
import functools
import math

import jax
import jax.numpy as jnp
from jax import lax
from jax.experimental import pallas as pl
from jax.experimental.pallas import tpu as pltpu
from jax.sharding import PartitionSpec as P

D = 1024
HEADS = 16
HD = 64
ROT = 16
LEN = 1024
DOCS = 4
FF = 4096
AXES = ("dp", "fsdp")
BLOCK = 512

feature_scale = 0.2
epsilon = 1e-05
precise = lax.Precision.HIGHEST
bf16 = jnp.bfloat16
f32 = jnp.float32
VMEM_LIMIT = 60 << 20


def cost(flops, transcendentals, bytes_accessed):
    return pl.CostEstimate(
        flops=flops * 4, transcendentals=transcendentals, bytes_accessed=bytes_accessed * 4
    )


class Grid:
    def __init__(self, dp, fsdp):
        self.dp, self.fsdp = dp, fsdp
        rest = fsdp // 2
        self.nx = 4 if rest % 16 == 0 else 2
        self.nz = rest // self.nx
        self.ny = dp
        self.n = dp * fsdp
        self.sizes = {"y": self.ny, "z": self.nz, "x": self.nx, "c": 2}
        self.stride = {"y": fsdp, "z": self.nx * 2, "x": 2, "c": 1}

    def digits(self):
        y = lax.axis_index("dp")
        f = lax.axis_index("fsdp")
        return {"y": y, "z": f // (self.nx * 2), "x": (f // 2) % self.nx, "c": f % 2}

    def swap(self, value, digit, k):
        stride = self.stride[digit]
        size = self.sizes[digit]
        pairs = []
        for i in range(self.n):
            d = (i // stride) % size
            pairs.append((i, i + ((d ^ k) - d) * stride))
        return lax.ppermute(value, AXES, pairs)

    def swap_by_core(self, value, digit_0, digit_1):
        flips = (self.stride[digit_0], self.stride[digit_1])
        return lax.ppermute(value, AXES, [(i, i ^ flips[i % 2]) for i in range(self.n)])


def place(pieces, outs, moves, after=()):
    n_in = len(pieces)
    n_out = len(outs)

    def body(*refs):
        ins, rest = refs[:n_in], refs[n_in + len(after) :]
        res, held, sem, done = rest[:n_out], rest[n_out : 2 * n_out], rest[-2], rest[-1]
        copies = []
        for i, (src, src_at, dst, dst_at) in enumerate(moves):
            copies.append(
                pltpu.make_async_copy(ins[src].at[src_at()], held[dst].at[dst_at()], sem.at[i])
            )
        for copy in copies:
            copy.start()
        back = []
        for o in range(n_out):
            for copy, move in zip(copies, moves):
                if move[2] == o:
                    copy.wait()
            back.append(pltpu.make_async_copy(held[o], res[o], done.at[o]))
            back[-1].start()
        for copy in back:
            copy.wait()

    total = sum(math.prod(o.shape) * o.dtype.itemsize for o in outs)
    return pl.pallas_call(
        body,
        out_shape=tuple(outs),
        in_specs=[pl.BlockSpec(memory_space=pl.ANY)] * (n_in + len(after)),
        out_specs=tuple([pl.BlockSpec(memory_space=pl.ANY)] * n_out),
        scratch_shapes=[pltpu.VMEM(o.shape, o.dtype) for o in outs]
        + [pltpu.SemaphoreType.DMA((len(moves),)), pltpu.SemaphoreType.DMA((n_out,))],
        compiler_params=pltpu.CompilerParams(vmem_limit_bytes=VMEM_LIMIT),
        cost_estimate=cost(flops=0, transcendentals=0, bytes_accessed=2 * total),
        name="place",
    )(*pieces, *after)


class Gather:
    def __init__(self, grid, both, fields, after=()):
        if after:
            both, *_ = lax.optimization_barrier((both, *after))
        self.grid, self.fields = grid, fields
        self.shape, self.dt = both.shape, both.dtype
        self.pieces = [both] + [grid.swap(both, "z", k) for k in range(1, grid.nz)]

    def first(self):
        g = self.grid
        outs = [jax.ShapeDtypeStruct((g.nz,) + self.shape, self.dt)]
        moves = [
            (k, lambda: (slice(None),), 0, lambda k=k: (g.digits()["z"] ^ k,)) for k in range(g.nz)
        ]
        return self.pieces, outs, moves, self.after_first

    def after_first(self, placed):
        self.pieces = [placed[0], self.grid.swap_by_core(placed[0], "x", "y")]

    def second(self):
        g = self.grid
        outs = [jax.ShapeDtypeStruct((2, g.nz) + self.shape, self.dt)]

        def dst_at(k):
            d = g.digits()
            return (jnp.where(d["c"] == 0, d["x"], d["y"]) ^ k,)

        moves = [(k, lambda: (slice(None),), 0, lambda k=k: dst_at(k)) for k in range(2)]
        return self.pieces, outs, moves, self.after_second

    def after_second(self, placed):
        self.pieces = [placed[0], self.grid.swap_by_core(placed[0], "y", "x")]

    def cores(self, after=()):
        pieces = tuple(self.pieces)
        if after:
            pieces = lax.optimization_barrier((*pieces, *after))[:2]
        self.pieces = list(pieces) + [self.grid.swap(piece, "c", 1) for piece in pieces]

    def third(self):
        g, rows = self.grid, self.shape[1]
        outs, moves = [], []
        first = 0
        for o, (cols, blocks) in enumerate(self.fields):
            wide = cols // blocks
            split = blocks == 1
            outs.append(
                jax.ShapeDtypeStruct(
                    (2, g.nz, 2, 2, 1 if split else 2 * blocks, rows, 2 * wide if split else wide), self.dt
                )
            )
            for p in range(4):
                for d1 in range(2):
                    for b in range(blocks):
                        start = first + b * wide

                        def src_at(d1=d1, start=start, wide=wide):
                            return (d1, slice(None), slice(None), slice(None), pl.ds(start, wide))

                        def dst_at(p=p, d1=d1, b=b, wide=wide, split=split, blocks=blocks):
                            d = g.digits()
                            half = d["c"] ^ (p // 2)
                            d2 = jnp.where(half == 0, d["y"], d["x"]) ^ (p % 2)
                            y = jnp.where(half == 0, d2, d1)
                            x = jnp.where(half == 0, d1, d2)
                            block = 0 if split else half * blocks + b
                            at = pl.ds(pl.multiple_of(half * wide, wide), wide) if split else slice(None)
                            return (y, slice(None), x, slice(None), block, slice(None), at)

                        moves.append((p, src_at, o, dst_at))
            first += cols
        return self.pieces, outs, moves, self.after_third

    def after_third(self, placed):
        self.full = [w.reshape(-1, w.shape[-1]) for w in placed]


def pack(grid, groups):
    core = grid.digits()["c"]
    halves = [[], []]
    for group in groups:
        for shard, _ in group:
            middle = shard.shape[1] // 2
            halves[0].append(shard[:, :middle])
            halves[1].append(shard[:, middle:])
    low, high = [jnp.concatenate(h, axis=1) for h in halves]
    mine, other = jnp.where(core == 0, low, high), jnp.where(core == 0, high, low)
    got = grid.swap(other, "c", 1)
    both = jnp.stack([jnp.where(core == 0, mine, got), jnp.where(core == 0, got, mine)])
    result = []
    at = 0
    for group in groups:
        cols = sum(shard.shape[1] // 2 for shard, _ in group)
        result.append((both[:, :, at : at + cols], [(s.shape[1] // 2, max(1, b // 2)) for s, b in group]))
        at += cols
    return result


def place_all(plans, after=()):
    pieces, outs, moves = [], [], []
    for p, o, m, _ in plans:
        moves += [(len(pieces) + src, src_at, len(outs) + dst, dst_at) for src, src_at, dst, dst_at in m]
        pieces += p
        outs += o
    placed = place(pieces, outs, moves, after)
    at = 0
    for _, o, _, done in plans:
        done(placed[at : at + len(o)])
        at += len(o)
    return list(placed[:1])


TILE = 256
WIDE = 256
PER = WIDE // HD
STEPS = LEN // TILE
GROUPS = HEADS // PER
PAIRS = [(q, k) for q in range(STEPS) for k in range(max(0, q - 2), q + 1)]


def nn(a, b):
    return lax.dot_general(a, b, (((1,), (0,)), ((), ())), preferred_element_type=f32)


def nt(a, b):
    return lax.dot_general(a, b, (((1,), (1,)), ((), ())), preferred_element_type=f32)


def halves(v):
    high = v.astype(bf16)
    return high, (v - high.astype(f32)).astype(bf16)


ANYWHERE = pl.BlockSpec(memory_space=pl.ANY)


def once(shape):
    return pl.BlockSpec(shape, lambda *g: (0,) * len(shape), pipeline_mode=pl.Buffered(1))


def norm_body(x_ref, gain_ref, shift_ref, hid_ref, hid_t_ref):
    x = x_ref[...].astype(f32)
    center = x - jnp.mean(x, axis=-1, keepdims=True)
    inv = lax.rsqrt(jnp.mean(center * center, axis=-1, keepdims=True) + epsilon)
    hid = center * inv * gain_ref[...] + shift_ref[...]
    hid_ref[...] = hid.astype(bf16)
    hid_t_ref[...] = hid.T.astype(bf16)


def norm(tokens, gain, shift):
    return pl.pallas_call(
        norm_body,
        grid=(STEPS,),
        out_shape=(jax.ShapeDtypeStruct((LEN, D), bf16), jax.ShapeDtypeStruct((D, LEN), bf16)),
        in_specs=[pl.BlockSpec((TILE, D), lambda g: (g, 0)), once((1, D)), once((1, D))],
        out_specs=(
            pl.BlockSpec((TILE, D), lambda g: (g, 0)),
            pl.BlockSpec((D, TILE), lambda g: (0, g)),
        ),
        compiler_params=pltpu.CompilerParams(vmem_limit_bytes=VMEM_LIMIT),
        cost_estimate=cost(flops=1 << 25, transcendentals=0, bytes_accessed=6 << 20),
        name="norm",
    )(tokens, gain, shift)


def attention_body(
    n_carried,
    core_ref,
    hid_ref,
    hid_t_ref,
    dy_ref,
    wq_ref,
    wk_ref,
    wv_ref,
    bq_ref,
    bk_ref,
    bv_ref,
    wo_ref,
    cos_ref,
    left_ref,
    right_ref,
    proj_ref,
    proj_low_ref,
    ones_ref,
    quad_ref,
    doc_col_ref,
    doc_row_ref,
    *rest,
):
    (
        att_ref,
        dm_ref,
        keep_ref,
        send_ref,
        keep_o_ref,
        send_o_ref,
        sums_ref,
        mask,
        scores,
        yq,
        yk,
        fq,
        fk,
        val,
        val_h,
        fq_t,
        dnum,
        dnum_t,
        cross,
        cross_low,
        att_t,
        num,
        den,
        dfq,
        dfk_t,
        dv_t,
        eq,
        ek,
    ) = rest[n_carried:]
    span = [pl.ds(r * TILE, TILE) for r in range(STEPS)]
    lane = lax.broadcasted_iota(jnp.int32, (TILE, WIDE), 1) // HD
    ones = ones_ref[...]
    proj, proj_low = proj_ref[...], proj_low_ref[...]

    for i, (q, k) in enumerate(PAIRS):
        here = doc_col_ref[span[q], :] == doc_row_ref[:, span[k]]
        if q == k:
            row = lax.broadcasted_iota(jnp.int32, (TILE, TILE), 0)
            col = lax.broadcasted_iota(jnp.int32, (TILE, TILE), 1)
            here = here & (row >= col)
        mask[i] = jnp.where(here, 1.0, 0.0).astype(bf16)

    hid = hid_ref[...]
    val[...] = (nn(hid, wv_ref[...]) + bv_ref[...]).astype(bf16)
    eq[...] = nn(hid, wq_ref[...]) + bq_ref[...]
    ek[...] = nn(hid, wk_ref[...]) + bk_ref[...]
    for r in range(STEPS):
        for y_out, f_out, e_out, scale in ((yq, fq, eq, True), (yk, fk, ek, False)):
            raw = e_out[span[r], :]
            y = (
                raw * cos_ref[span[r], :]
                + pltpu.roll(raw, WIDE - 8, 1) * left_ref[span[r], :]
                + pltpu.roll(raw, 8, 1) * right_ref[span[r], :]
            )
            y_high, y_low = halves(y)
            s_high, s_low = halves(y * y)
            power = nt(y_high, proj) + nt(y_low, proj) + nt(y_high, proj_low)
            power = power - 0.5 * (nn(s_high, ones) + nn(s_low, ones))
            feat = jnp.exp(power)
            if scale:
                feat = feat * quad_ref[...]
            y_out[span[r], :] = y
            e_out[span[r], :] = feat
            f_out[span[r], :] = feat.astype(bf16)
            if scale:
                fq_t[:, span[r]] = feat.T.astype(bf16)

    def forward(h, carry):
        own = lane == h
        for r in range(STEPS):
            val_h[h, span[r], :] = jnp.where(own, val[span[r], :], jnp.ones((), bf16))
        total = None
        for i, (q, k) in enumerate(PAIRS):
            query = jnp.where(own, fq[span[q], :], jnp.zeros((), bf16))
            tile = nt(query, fk[span[k], :]).astype(bf16) * mask[i]
            scores[h * len(PAIRS) + i] = tile
            part = nn(tile, val_h[h, span[k], :])
            total = part if total is None else total + part
            if k == q:
                num[span[q], :] = jnp.where(own, total, num[span[q], :])
                den[span[q], :] = jnp.where(own, pltpu.roll(total, HD, 1), den[span[q], :])
                total = None
        return carry

    lax.fori_loop(0, PER, forward, 0, unroll=True)

    dfq[...] = nt(dy_ref[...], wo_ref[...])
    for r in range(STEPS):
        grad = dfq[span[r], :]
        inv = 1.0 / den[span[r], :]
        att = num[span[r], :] * inv
        att_ref[span[r], :] = att.astype(bf16)
        d_num = grad * inv
        dnum[span[r], :] = d_num.astype(bf16)
        dnum_t[:, span[r]] = d_num.T.astype(bf16)
        att_t[:, span[r]] = att.T.astype(bf16)
        high, low = halves(pltpu.roll(-d_num * att, HD, 1))
        cross[span[r], :] = high
        cross_low[span[r], :] = pltpu.roll(low.astype(f32), HD, 1).astype(bf16)

    def backward(h, carry):
        own = lane == h
        after = lane == lax.rem(h + 1, PER)
        later = lane == lax.rem(h + 2, PER)
        mine = pl.ds(pl.multiple_of(h * HD, HD), HD)
        dfk_t[mine, :] = jnp.zeros((HD, LEN), f32)
        dv_t[mine, :] = jnp.zeros((HD, LEN), f32)
        total = None
        for i, (q, k) in enumerate(PAIRS):
            left = jnp.where(
                own,
                dnum[span[q], :],
                jnp.where(
                    after,
                    cross[span[q], :],
                    jnp.where(later, cross_low[span[q], :], jnp.zeros((), bf16)),
                ),
            )
            tile = nt(left, val_h[h, span[k], :]).astype(bf16) * mask[i]
            part = nn(tile, fk[span[k], :])
            total = part if total is None else total + part
            dfk_t[mine, span[k]] += nn(fq_t[mine, span[q]], tile)
            dv_t[mine, span[k]] += nn(dnum_t[mine, span[q]], scores[h * len(PAIRS) + i])
            if k == q:
                dfq[span[q], :] = jnp.where(own, total, dfq[span[q], :])
                total = None
        return carry

    lax.fori_loop(0, PER, backward, 0, unroll=True)

    sums = [jnp.zeros((1, WIDE), f32)] * 3
    for r in range(STEPS):
        grads = []
        for d_feat, feat, y in (
            (dfq[span[r], :], eq, yq),
            (dfk_t[:, span[r]].T, ek, yk),
        ):
            e_high, e_low = halves(d_feat * feat[span[r], :])
            d_y = nn(e_high, proj) + nn(e_low, proj) + nn(e_high, proj_low)
            d_y = d_y - (nn(e_high, ones) + nn(e_low, ones)) * y[span[r], :]
            grads.append(
                d_y * cos_ref[span[r], :]
                - pltpu.roll(d_y, WIDE - 8, 1) * left_ref[span[r], :]
                - pltpu.roll(d_y, 8, 1) * right_ref[span[r], :]
            )
        grads.append(dv_t[:, span[r]].T)
        for i in range(3):
            low = grads[i].astype(bf16)
            dm_ref[i, span[r], :] = low
            sums[i] = sums[i] + jnp.sum(low.astype(f32), axis=0, keepdims=True)
    for i in range(3):
        sums_ref[pl.ds(i, 1), :] = sums[i]

    first = core_ref[0] == 0
    half = WIDE // 2
    for i in range(3):
        full = nn(hid_t_ref[...], dm_ref[i]).astype(bf16)
        low, high = full[:, :half], full[:, half:]
        keep_ref[i] = jnp.where(first, low, high)
        send_ref[i] = jnp.where(first, high, low)
    full = nn(att_t[...], dy_ref[...]).astype(bf16)
    low, high = full[:, : D // 2], full[:, D // 2 :]
    keep_o_ref[...] = jnp.where(first, low, high)
    send_o_ref[...] = jnp.where(first, high, low)


def attention(core, group, operands, w_qkv, w_out, carried, after):
    hid, hid_t, dy, b_qkv, cos_t, left_t, right_t, proj, proj_low, ones, quad, doc_col, doc_row = operands
    half = D // 2
    at = lambda shape, index: pl.BlockSpec(shape, lambda s: index, pipeline_mode=pl.Buffered(1))
    col = lambda part: at((D, WIDE), (0, part * 2 + group % 2))
    bias = lambda part: at((1, WIDE), (0, part * GROUPS + group))
    shapes = [
        ((LEN, D), bf16, at((LEN, WIDE), (0, group))),
        ((3, LEN, D), bf16, at((3, LEN, WIDE), (0, 0, group))),
        ((3, D, half), bf16, at((3, D, WIDE // 2), (0, 0, group))),
        ((3, D, half), bf16, at((3, D, WIDE // 2), (0, 0, group))),
        ((D, half), bf16, at((WIDE, half), (group, 0))),
        ((D, half), bf16, at((WIDE, half), (group, 0))),
        ((8, D), f32, at((8, WIDE), (0, group))),
    ]
    in_specs = [
        pl.BlockSpec(memory_space=pltpu.SMEM),
        once((LEN, D)),
        once((D, LEN)),
        once((LEN, D)),
        col(0),
        col(1),
        col(2),
        bias(0),
        bias(1),
        bias(2),
        at((WIDE, D), (group, 0)),
        once((LEN, WIDE)),
        once((LEN, WIDE)),
        once((LEN, WIDE)),
        once((WIDE, WIDE)),
        once((WIDE, WIDE)),
        once((WIDE, WIDE)),
        once((1, WIDE)),
        once((LEN, 1)),
        once((1, LEN)),
    ]
    extra = list(carried) + list(after)
    vm = pltpu.VMEM
    tall, flat = (LEN, WIDE), (WIDE, LEN)
    scratch = [
        vm((len(PAIRS), TILE, TILE), bf16),
        vm((PER * len(PAIRS), TILE, TILE), bf16),
        vm(tall, f32),
        vm(tall, f32),
        vm(tall, bf16),
        vm(tall, bf16),
        vm(tall, bf16),
        vm((PER,) + tall, bf16),
        vm(flat, bf16),
        vm(tall, bf16),
        vm(flat, bf16),
        vm(tall, bf16),
        vm(tall, bf16),
        vm(flat, bf16),
        vm(tall, f32),
        vm(tall, f32),
        vm(tall, f32),
        vm(flat, f32),
        vm(flat, f32),
        vm(tall, f32),
        vm(tall, f32),
    ]
    return pl.pallas_call(
        functools.partial(attention_body, len(extra)),
        grid=(1,),
        out_shape=tuple(jax.ShapeDtypeStruct(s, t) for s, t, _ in shapes),
        in_specs=in_specs + [ANYWHERE] * len(extra),
        out_specs=tuple(spec for _, _, spec in shapes),
        scratch_shapes=scratch,
        input_output_aliases={len(in_specs) + i: i for i in range(len(carried))},
        compiler_params=pltpu.CompilerParams(vmem_limit_bytes=VMEM_LIMIT),
        cost_estimate=cost(flops=30 << 30, transcendentals=0, bytes_accessed=20 << 20),
        name="attention",
    )(
        core, hid, hid_t, dy, w_qkv, w_qkv, w_qkv, b_qkv, b_qkv, b_qkv, w_out,
        cos_t, left_t, right_t, proj, proj_low, ones, quad, doc_col, doc_row, *extra,
    )


CALLS = 2


def up_body(rows, wide, n_extra, core_ref, hid_ref, dy_ref, w1_ref, b1_ref, *rest):
    act_ref, slope_ref, keep_ref, send_ref, act_t = rest[n_extra:]
    block = w1_ref.shape[1]
    for r in range(STEPS):
        at = pl.ds(r * TILE, TILE)
        upper = nn(hid_ref[at, :], w1_ref[...]) + b1_ref[...]
        bell = jnp.exp(-0.5 * upper * upper)
        phi = 0.5 + 0.5 * lax.erf(upper * (1.0 / math.sqrt(2.0)))
        act = (upper * phi).astype(bf16)
        act_ref[at, :] = act
        act_t[:, at] = act.T
        slope_ref[at, :] = (phi + upper * bell * (1.0 / math.sqrt(2.0 * math.pi))).astype(bf16)
    first = core_ref[0] == 0
    full = nn(act_t[...], dy_ref[...]).astype(bf16)
    top = wide // rows // 2
    for p in range(block // wide):
        for b in range(top):
            low = full[p * wide + b * rows : p * wide + (b + 1) * rows]
            start = p * wide + (top + b) * rows
            high = full[start : start + rows]
            keep_ref[b, pl.ds(p * rows, rows), :] = jnp.where(first, low, high)
            send_ref[b, pl.ds(p * rows, rows), :] = jnp.where(first, high, low)


def up_part(core, rows, wide, call, hid, dy, w1, b1, carried=(), after=()):
    grid = FF // BLOCK // CALLS
    base = call * grid
    top = wide // rows // 2
    per = BLOCK // wide * rows
    total = FF // wide * rows
    grad = ((top, total, D), bf16, pl.BlockSpec((top, per, D), lambda g: (0, base + g, 0)))
    units = ((LEN, FF), bf16, pl.BlockSpec((LEN, BLOCK), lambda g: (0, base + g)))
    shapes = [units, units, grad, grad]
    extra = list(carried) + list(after)
    return pl.pallas_call(
        functools.partial(up_body, rows, wide, len(extra)),
        grid=(grid,),
        out_shape=tuple(jax.ShapeDtypeStruct(s, t) for s, t, _ in shapes),
        in_specs=[
            pl.BlockSpec(memory_space=pltpu.SMEM),
            once((LEN, D)),
            once((LEN, D)),
            pl.BlockSpec((D, BLOCK), lambda g: (0, base + g)),
            pl.BlockSpec((1, BLOCK), lambda g: (0, base + g)),
        ]
        + [ANYWHERE] * len(extra),
        out_specs=tuple(spec for _, _, spec in shapes),
        scratch_shapes=[pltpu.VMEM((BLOCK, LEN), bf16)],
        input_output_aliases={5 + i: i for i in range(len(carried))},
        compiler_params=pltpu.CompilerParams(vmem_limit_bytes=VMEM_LIMIT),
        cost_estimate=cost(
            flops=4 * LEN * D * FF // CALLS, transcendentals=0, bytes_accessed=18 << 20
        ),
        name="up",
    )(core, hid, dy, w1, b1, *extra)


def down_body(n_extra, core_ref, hid_t_ref, dy_ref, w2_ref, slope_ref, *rest):
    dup_ref, sums_ref, grad_ref = rest[n_extra:]
    block = w2_ref.shape[0]
    total = jnp.zeros((1, block), f32)
    for r in range(STEPS):
        at = pl.ds(r * TILE, TILE)
        d_up = (nt(dy_ref[at, :], w2_ref[...]) * slope_ref[at, :].astype(f32)).astype(bf16)
        dup_ref[at, :] = d_up
        total = total + jnp.sum(d_up.astype(f32), axis=0, keepdims=True)
    sums_ref[...] = total
    grad_ref[0] = nn(hid_t_ref[...], dup_ref[...]).astype(bf16)


def down_part(core, call, hid_t, dy, w2, slope, carried=(), after=()):
    grid = FF // BLOCK // CALLS
    per = D // BLOCK
    unit = lambda g, ref: (ref[0] ^ 1 ^ call) * grid + g
    shapes = [
        ((LEN, FF), bf16, pl.BlockSpec((LEN, BLOCK), lambda g, ref: (0, unit(g, ref)))),
        ((1, FF), f32, pl.BlockSpec((1, BLOCK), lambda g, ref: (0, unit(g, ref)))),
        (
            (FF // D // CALLS, D, D),
            bf16,
            pl.BlockSpec((1, D, BLOCK), lambda g, ref: (g // per, 0, g % per)),
        ),
    ]
    extra = list(carried) + list(after)
    return pl.pallas_call(
        functools.partial(down_body, len(extra)),
        grid_spec=pltpu.PrefetchScalarGridSpec(
            num_scalar_prefetch=1,
            grid=(grid,),
            in_specs=[
                once((D, LEN)),
                once((LEN, D)),
                pl.BlockSpec((BLOCK, D), lambda g, ref: (unit(g, ref), 0)),
                pl.BlockSpec((LEN, BLOCK), lambda g, ref: (0, unit(g, ref))),
            ]
            + [ANYWHERE] * len(extra),
            out_specs=tuple(spec for _, _, spec in shapes),
        ),
        out_shape=tuple(jax.ShapeDtypeStruct(s, t) for s, t, _ in shapes),
        input_output_aliases={5 + i: i for i in range(len(carried))},
        compiler_params=pltpu.CompilerParams(vmem_limit_bytes=VMEM_LIMIT),
        cost_estimate=cost(
            flops=4 * LEN * D * FF // CALLS, transcendentals=0, bytes_accessed=18 << 20
        ),
        name="down",
    )(core, hid_t, dy, w2, slope, *extra)


CHUNK = 512


def output_first_body(n_after, act_ref, w2_ref, x_ref, bias_ref, *rest):
    out_ref = rest[n_after]

    @pl.when(pl.program_id(0) == 0)
    def _():
        out_ref[...] = x_ref[...].astype(f32) + bias_ref[...]

    out_ref[...] += nn(act_ref[...], w2_ref[...])


def output_first(act, w2, tokens, bias, after=()):
    return pl.pallas_call(
        functools.partial(output_first_body, len(after)),
        grid=(FF // CHUNK // 2,),
        out_shape=jax.ShapeDtypeStruct((LEN, D), f32),
        in_specs=[
            pl.BlockSpec((LEN, CHUNK), lambda g: (0, g)),
            pl.BlockSpec((CHUNK, D), lambda g: (g, 0)),
            once((LEN, D)),
            once((1, D)),
        ]
        + [ANYWHERE] * len(after),
        out_specs=once((LEN, D)),
        compiler_params=pltpu.CompilerParams(vmem_limit_bytes=VMEM_LIMIT),
        cost_estimate=cost(
            flops=LEN * D * FF, transcendentals=0, bytes_accessed=14 << 20
        ),
        name="output_first",
    )(act, w2, tokens, bias, *after)


def output_rest_body(n_after, act_ref, att_ref, w2_ref, wo_ref, acc_ref, *rest):
    out_ref = rest[n_after]
    step = pl.program_id(0)

    @pl.when(step == 0)
    def _():
        out_ref[...] = acc_ref[...] + nn(act_ref[...], w2_ref[...])

    @pl.when((step > 0) & (step < FF // CHUNK // 2))
    def _():
        out_ref[...] += nn(act_ref[...], w2_ref[...])

    @pl.when(step >= FF // CHUNK // 2)
    def _():
        out_ref[...] += nn(att_ref[...], wo_ref[...])


def output_rest(act, att, w2, wo, acc, after=()):
    lead, tail = FF // CHUNK // 2, D // CHUNK
    low = lambda g: lead + jnp.minimum(g, lead - 1)
    high = lambda g: jnp.maximum(g - lead, 0)
    return pl.pallas_call(
        functools.partial(output_rest_body, len(after)),
        grid=(lead + tail,),
        out_shape=jax.ShapeDtypeStruct((LEN, D), f32),
        in_specs=[
            pl.BlockSpec((LEN, CHUNK), lambda g: (0, low(g))),
            pl.BlockSpec((LEN, CHUNK), lambda g: (0, high(g))),
            pl.BlockSpec((CHUNK, D), lambda g: (low(g), 0)),
            pl.BlockSpec((CHUNK, D), lambda g: (high(g), 0)),
            once((LEN, D)),
        ]
        + [ANYWHERE] * len(after),
        out_specs=once((LEN, D)),
        compiler_params=pltpu.CompilerParams(vmem_limit_bytes=VMEM_LIMIT),
        cost_estimate=cost(
            flops=LEN * D * (FF + 2 * D), transcendentals=0, bytes_accessed=18 << 20
        ),
        name="output_rest",
    )(act, att, w2, wo, acc, *after)


def back_body(n_after, dup_ref, w1_ref, *rest):
    acc_ref = rest[n_after]
    step = pl.program_id(0)

    @pl.when(step == 0)
    def _():
        acc_ref[...] = nt(dup_ref[...], w1_ref[...])

    @pl.when(step > 0)
    def _():
        acc_ref[...] += nt(dup_ref[...], w1_ref[...])


def back_part(d_up, w1, after=()):
    return pl.pallas_call(
        functools.partial(back_body, len(after)),
        grid=(FF // CHUNK,),
        out_shape=jax.ShapeDtypeStruct((LEN, D), f32),
        in_specs=[
            pl.BlockSpec((LEN, CHUNK), lambda g: (0, g)),
            pl.BlockSpec((D, CHUNK), lambda g: (0, g)),
        ]
        + [ANYWHERE] * len(after),
        out_specs=once((LEN, D)),
        compiler_params=pltpu.CompilerParams(vmem_limit_bytes=VMEM_LIMIT),
        cost_estimate=cost(
            flops=2 * LEN * D * FF, transcendentals=0, bytes_accessed=20 << 20
        ),
        name="back",
    )(d_up, w1, *after)


def input_body(n_after, dm_ref, wa_ref, wb_ref, acc_ref, x_ref, cot_ref, gain_ref, *rest):
    out_ref, sums_ref, acc = rest[n_after:]
    step = pl.program_id(0)
    last = 3 * D // CHUNK - 1

    @pl.when(step == 0)
    def _():
        acc[...] = acc_ref[...] + nt(dm_ref[0], wa_ref[...])

    @pl.when((step > 0) & (step < 3))
    def _():
        acc[...] += nt(dm_ref[0], wa_ref[...])

    @pl.when(step >= 3)
    def _():
        acc[...] += nt(dm_ref[0], wb_ref[...])

    @pl.when(step == last)
    def _():
        g_gain, g_shift = jnp.zeros((1, D), f32), jnp.zeros((1, D), f32)
        for r in range(STEPS):
            at = pl.ds(r * TILE, TILE)
            x = x_ref[at, :].astype(f32)
            center = x - jnp.mean(x, axis=-1, keepdims=True)
            inv = lax.rsqrt(jnp.mean(center * center, axis=-1, keepdims=True) + epsilon)
            normed = center * inv
            d_hidden = acc[at, :]
            g_gain = g_gain + jnp.sum(d_hidden * normed, axis=0, keepdims=True)
            g_shift = g_shift + jnp.sum(d_hidden, axis=0, keepdims=True)
            d_normed = d_hidden * gain_ref[...]
            mean_grad = jnp.mean(d_normed, axis=-1, keepdims=True)
            mean_cross = jnp.mean(d_normed * normed, axis=-1, keepdims=True)
            out_ref[at, :] = cot_ref[at, :] + inv * (d_normed - mean_grad - normed * mean_cross)
        sums_ref[0:1, :] = g_gain
        sums_ref[1:2, :] = g_shift


def input_part(d_mixed, wa, wb, acc, tokens, cotangent, gain, after=()):
    per = D // CHUNK
    return pl.pallas_call(
        functools.partial(input_body, len(after)),
        grid=(3 * per,),
        out_shape=(jax.ShapeDtypeStruct((LEN, D), f32), jax.ShapeDtypeStruct((8, D), f32)),
        in_specs=[
            pl.BlockSpec((1, LEN, CHUNK), lambda g: (g % 3, 0, g // 3)),
            pl.BlockSpec((D, CHUNK), lambda g: (0, jnp.minimum(g, 2))),
            pl.BlockSpec((D, CHUNK), lambda g: (0, jnp.maximum(g - 3, 0))),
            once((LEN, D)),
            once((LEN, D)),
            once((LEN, D)),
            once((1, D)),
        ]
        + [ANYWHERE] * len(after),
        out_specs=(once((LEN, D)), once((8, D))),
        scratch_shapes=[pltpu.VMEM((LEN, D), f32)],
        compiler_params=pltpu.CompilerParams(vmem_limit_bytes=VMEM_LIMIT),
        cost_estimate=cost(
            flops=6 * LEN * D * D, transcendentals=0, bytes_accessed=32 << 20
        ),
        name="input",
    )(d_mixed, wa, wb, acc, tokens, cotangent, gain, *after)


def fold(terms, view, block, in_at, out_view, out_block, out_at, n, steps, scalars, after=()):
    args, in_specs, out_specs, shapes, plan = [], [], [], [], []
    count = sum(part.shape[0] for part in terms[0])
    for j in range(n):
        sources = []
        for term in terms:
            spans = []
            at = 0
            for part in term:
                k = part.shape[0]
                spans.append((len(args), at, k))
                args.append(part.reshape((k,) + view))
                in_specs.append(
                    pl.BlockSpec((k,) + block, lambda s, ref, j=j: (0,) + in_at(s, j, ref))
                )
                at += k
            sources.append(spans)
        plan.append(sources)
        out_specs.append(pl.BlockSpec((count,) + out_block, lambda s, ref: (0,) + out_at(s)))
        shapes.append(jax.ShapeDtypeStruct((count,) + out_view, bf16))
    n_args = len(args)
    n_after = len(after)
    moved = n * (len(terms) + 1) * 2 * count * math.prod(out_view)

    def body(ref, *refs):
        for o, sources in enumerate(plan):
            out = refs[n_args + n_after + o]
            cuts = sorted({cut for spans in sources for _, at, k in spans for cut in (at, at + k)})
            for lo, hi in zip(cuts, cuts[1:]):
                total = None
                for spans in sources:
                    for arg, at, k in spans:
                        if at <= lo and hi <= at + k:
                            value = refs[arg][lo - at : hi - at].astype(f32)
                            total = value if total is None else total + value
                out[lo:hi] = total.astype(bf16).reshape((hi - lo,) + out_block)

    return list(
        pl.pallas_call(
            body,
            grid_spec=pltpu.PrefetchScalarGridSpec(
                num_scalar_prefetch=1,
                grid=(steps,),
                in_specs=in_specs + [ANYWHERE] * n_after,
                out_specs=out_specs,
            ),
            out_shape=tuple(shapes),
            compiler_params=pltpu.CompilerParams(vmem_limit_bytes=VMEM_LIMIT),
            cost_estimate=cost(flops=moved, transcendentals=0, bytes_accessed=moved),
            name="fold",
        )(scalars, *args, *after)
    )


class Reduction:
    def __init__(self, grid, keep, send):
        self.grid = grid
        self.d = d = grid.digits()
        first = d["c"] == 0
        self.own = jnp.where(first, d["x"], d["y"]).astype(jnp.int32)
        self.next = jnp.where(first, d["y"], d["x"]).astype(jnp.int32)
        self.cols = keep[0].shape[-1]
        self.rows = keep[0].shape[1] // grid.n
        self.terms = [keep, [grid.swap(v, "c", 1) for v in send]]

    def token(self):
        return self.terms[0]

    def first(self, after=()):
        g, cols, two = self.grid, self.cols, 2 * self.rows
        half = cols // 2

        def in_at(s, j, ref):
            mine, other = ref[1] ^ j, s // 2
            y = jnp.where(ref[0] == 0, other, mine)
            x = jnp.where(ref[0] == 0, mine, other)
            return (y, 0, x, 0, s % 2)

        parts = fold(
            self.terms,
            (2, g.nz, 2, two, cols),
            (1, g.nz, 1, two, half),
            in_at,
            (2, g.nz, two, cols),
            (1, g.nz, two, half),
            lambda s: (s // 2, 0, 0, s % 2),
            2,
            4,
            jnp.stack([self.d["c"].astype(jnp.int32), self.own]),
            after,
        )
        self.terms = [parts[:1], [g.swap_by_core(parts[1], "x", "y")]]

    def second(self, after=()):
        g, cols, two = self.grid, self.cols, 2 * self.rows
        part = cols // 4
        parts = fold(
            self.terms,
            (2, g.nz, two, cols),
            (1, g.nz, two, part),
            lambda s, j, ref: (ref[0] ^ j, 0, 0, s),
            (g.nz, two, cols),
            (g.nz, two, part),
            lambda s: (0, 0, s),
            2,
            4,
            self.next[None],
            after,
        )
        self.terms = [parts[:1], [g.swap_by_core(parts[1], "y", "x")]]

    def third(self, after=()):
        g, cols, two = self.grid, self.cols, 2 * self.rows
        part = cols // 2
        parts = fold(
            self.terms,
            (g.nz, two, cols),
            (1, two, part),
            lambda s, j, ref: (ref[0] ^ j, 0, s),
            (two, cols),
            (two, part),
            lambda s: (0, s),
            g.nz,
            2,
            self.d["z"].astype(jnp.int32)[None],
            after,
        )
        self.parts = [parts[0]] + [g.swap(parts[j], "z", j) for j in range(1, g.nz)]

    def result(self, after=()):
        if after:
            self.parts = lax.optimization_barrier((*self.parts, *after))[: len(self.parts)]
        total = self.parts[0].astype(f32)
        for part in self.parts[1:]:
            total = total + part.astype(f32)
        total = total.reshape(-1, 2, self.rows, self.cols)
        core = self.d["c"]
        mine = pick(total, 1, core)
        got = self.grid.swap(pick(total, 1, 1 - core), "c", 1)
        return jnp.where(core == 0, mine, got), jnp.where(core == 0, got, mine)


class SmallReduction:
    def __init__(self, grid, grad):
        self.grid = grid
        self.d = grid.digits()
        self.now = grad.reshape(grid.ny, grid.nz, grid.nx, 2, grad.shape[1])

    def step(self, digit, axis, after=None):
        if after is not None:
            self.now, _ = lax.optimization_barrier((self.now, after))
        mine = pick(self.now, axis, self.d[digit])
        for k in range(1, self.grid.sizes[digit]):
            mine = mine + self.grid.swap(pick(self.now, axis, self.d[digit] ^ k), digit, k)
        self.now = mine

    def last(self):
        self.step("z", 0)
        return self.now


def tables(node_seeds, node_weights):
    width = node_seeds.shape[1]
    uniform_pts = (node_seeds.astype(jnp.float32) + 0.5) / 1024.0
    nodes = math.sqrt(2.0) * lax.erf_inv(2.0 * uniform_pts - 1.0)
    order = jnp.arange(width).astype(jnp.float32)
    scales = jnp.where(order[:, None] == 0.0, math.sqrt(1.0 / width), math.sqrt(2.0 / width))
    basis = scales * jnp.cos(
        math.pi * (2.0 * order[None, :] + 1.0) * order[:, None] / (2.0 * width)
    )
    projection = jnp.dot(nodes, basis, precision=precise)
    weights_float = node_weights.astype(jnp.float32)
    return (projection, weights_float / jnp.sum(weights_float))


def layout(lengths):
    ends = jnp.cumsum(lengths)
    starts = ends - lengths
    places = jnp.arange(LEN, dtype=jnp.int32)
    doc_ids = jnp.sum((places[:, None] >= ends[None, :]).astype(jnp.int32), axis=1)
    owners = doc_ids[:, None] == jnp.arange(DOCS, dtype=jnp.int32)[None, :]
    begins = jnp.sum(jnp.where(owners, starts[None, :], 0), axis=1)
    return (doc_ids, (places - begins).astype(jnp.float32))


def rotary(positions):
    half_rot = ROT // 2
    freqs = 10000.0 ** (-2.0 * jnp.arange(half_rot).astype(jnp.float32) / ROT)
    angles = positions[:, None] * freqs[None, :]
    return (jnp.cos(angles), jnp.sin(angles))


def pick(value, axis, index):
    return lax.dynamic_index_in_dim(value, index, axis, keepdims=False)


def shards(
    grid,
    tokens,
    ln_gain,
    ln_bias,
    qkv_weight,
    qkv_bias,
    out_weight,
    out_bias,
    fc1_weight,
    fc1_bias,
    fc2_weight,
    fc2_bias,
    cotangent,
    doc_lengths,
    node_seeds,
    node_weights,
):
    n = grid.n
    rows = qkv_weight.shape[0]
    staged = rows % 32 == 0 and grid.nx == 2 and grid.ny == 2
    block_rows = rows if staged else 32
    wide = FF // n if staged else 64
    folds = wide // block_rows
    vectors = (ln_gain, ln_bias, qkv_bias, out_bias, fc1_bias, fc2_bias)
    small = jnp.concatenate(vectors)
    per_row = small.shape[0] // rows
    small = jnp.pad(small.reshape(rows, per_row), ((0, 0), (0, 128 - per_row)))
    if staged:
        pairs = [
            jnp.concatenate([qkv_weight[:, p * D + h : p * D + h + D // 2] for p in range(3)], axis=1)
            for h in (0, D // 2)
        ]
        folded = fc2_weight.reshape(folds, rows, D)
        folded = jnp.concatenate([folded[i] for i in range(folds)], axis=1)
        packed = pack(
            grid,
            [
                [(pairs[0], 1), (out_weight, 1), (jnp.pad(small, ((0, 0), (0, 128))), 1)],
                [(pairs[1], 1)],
                [(fc1_weight, 1)],
                [(folded, folds)],
            ],
        )
        head = Gather(grid, *packed[0])
        token = place_all([head.first()])
        rest = Gather(grid, *packed[1], token)
        token = place_all([head.second(), rest.first()])
        head.cores()
        ups = Gather(grid, *packed[2], token)
        place_all([head.third()])
        pair_weights, attn_weight, small_all = [head.full[0], None], head.full[1], head.full[2]
    else:
        joint_weight, small_all, attn_weight, up_weight, down_weight = [
            lax.all_gather(w, AXES, axis=0, tiled=True)
            for w in (qkv_weight, small, out_weight, fc1_weight, fc2_weight)
        ]
        pair_weights = [
            jnp.concatenate([joint_weight[:, p * D + h : p * D + h + D // 2] for p in range(3)], axis=1)
            for h in (0, D // 2)
        ]
    small_all = small_all[:, :per_row].reshape(n, rows * per_row)
    whole = []
    at = 0
    for v in vectors:
        whole.append(small_all[:, at : at + v.shape[0]].reshape(n * v.shape[0]).astype(f32))
        at += v.shape[0]
    norm_gain, norm_shift, joint_bias, attn_bias, up_bias, down_bias = whole

    core = grid.digits()["c"] if staged else jnp.zeros((), jnp.int32)
    core_arg = core.reshape(1).astype(jnp.int32)
    dy_low = cotangent.astype(bf16)
    dy_sums = jnp.sum(dy_low.astype(f32), axis=0)
    hidden_low, hidden_t = norm(tokens, norm_gain[None], norm_shift[None])

    projection, quad = tables(node_seeds, node_weights)
    doc_ids, positions = layout(doc_lengths[0])
    cos, sin = rotary(positions)
    flat = jnp.ones((LEN, HD - ROT), f32)
    none = jnp.zeros((LEN, ROT // 2), f32)
    cos_t = feature_scale * jnp.tile(jnp.concatenate([cos, cos, flat], axis=1), (1, PER))
    left_t = feature_scale * jnp.tile(jnp.concatenate([-sin, none, 0 * flat], axis=1), (1, PER))
    right_t = feature_scale * jnp.tile(jnp.concatenate([none, sin, 0 * flat], axis=1), (1, PER))
    eye = jnp.eye(PER, dtype=f32)
    wide_proj = jnp.einsum("ab,jd->ajbd", eye, projection, precision=precise).reshape(WIDE, WIDE)
    near = lax.reduce_precision(wide_proj, 8, 7)
    ones = jnp.kron(eye, jnp.ones((HD, HD), f32)).astype(bf16)

    operands = (
        hidden_low,
        hidden_t,
        dy_low,
        joint_bias[None],
        cos_t,
        left_t,
        right_t,
        near.astype(bf16),
        (wide_proj - near).astype(bf16),
        ones,
        jnp.tile(quad, PER)[None],
        doc_ids[:, None],
        doc_ids[None],
    )
    carried = ()
    for group in range(GROUPS):
        after = ()
        if staged and group == 1:
            token = place_all([rest.second(), ups.first()], carried[:1])
            after = token
        if staged and group == 2:
            rest.cores(carried[:1])
            place_all([rest.third(), ups.second()])
            pair_weights[1] = rest.full[0]
            downs = Gather(grid, *packed[3], (rest.full[0],))
        if staged and group == 3:
            ups.cores(carried[:1])
            token = place_all([ups.third(), downs.first()], carried[:1])
            up_weight = ups.full[0]
            after = token
        carried = attention(
            core_arg, group, operands, pair_weights[group // 2], attn_weight, carried, after
        )
    att, d_mixed, keep_qkv, send_qkv, keep_o, send_o, joint_sums = carried
    after = carried[:1]
    if staged:
        joint_sum = Reduction(grid, [keep_qkv, keep_o[None]], [send_qkv, send_o[None]])
        after = place_all([downs.second()], carried[:1])
    hidden = ()
    for call in range(CALLS):
        if staged and call == 1:
            joint_sum.first(hidden[:1])
            after = joint_sum.token()
        hidden = up_part(
            core_arg, block_rows, wide, call, hidden_low, dy_low, up_weight, up_bias[None], hidden, after
        )
    act, slope, keep_2, send_2 = hidden
    after = hidden[:1]
    if staged:
        downs.cores(hidden[:1])
        joint_sum.second(hidden[:1])
        place_all([downs.third()], joint_sum.token())
        (down_weight,) = downs.full
        down_sum = Reduction(grid, [keep_2], [send_2])
    back = ()
    grads_1 = []
    for call in range(CALLS):
        if staged and call == 1:
            joint_sum.third(back[:1])
            down_sum.first(joint_sum.parts[:1])
            after = down_sum.token()
        d_up, up_sums, grad = down_part(
            core_arg, call, hidden_t, dy_low, down_weight, slope, back, after
        )
        back = (d_up, up_sums)
        grads_1.append(grad)
    after = ()
    if staged:
        up_sum = Reduction(grid, grads_1[1:], grads_1[:1])
        down_sum.second(back[:1])
        after = down_sum.token()
    d_hidden = back_part(d_up, up_weight, after)
    bias = (attn_bias + down_bias)[None]
    g_up_bias = up_sums.reshape(FF)
    g_joint_bias = joint_sums[:3].reshape(3 * D)
    after = ()
    if staged:
        up_sum.first([d_hidden])
        total = joint_sum.result([d_hidden])
        down_sum.third(up_sum.token())
        after = down_sum.parts[:1]
    input_grad, norm_sums = input_part(
        d_mixed, *pair_weights, d_hidden, tokens, cotangent, norm_gain[None], after
    )
    grads = (norm_sums[0], norm_sums[1], g_joint_bias, dy_sums, g_up_bias)
    packed = jnp.concatenate([g.reshape(n, -1) for g in grads], axis=1)
    after = ()
    if staged:
        up_sum.second([input_grad])
        small_sum = SmallReduction(grid, packed)
        small_sum.step("c", 3)
        after = up_sum.token()
    output = output_first(act, down_weight, tokens, bias, after)
    if staged:
        down_total = down_sum.result([output])
        small_sum.step("x", 2, output)
        up_sum.third([output])
        after = up_sum.parts[:1]
    output = output_rest(act, att, down_weight, attn_weight, output, after)
    if staged:
        small_sum.step("y", 0, output)
        s_small = small_sum.last()
        up_total = up_sum.result([output])
        both = jnp.stack([h[:3].reshape(3, rows, GROUPS, WIDE // 2) for h in total], axis=3)
        both = both.reshape(3, rows, D)
        s_joint = jnp.concatenate([both[0], both[1], both[2]], axis=1)
        s_attn = jnp.concatenate([h[3] for h in total], axis=1)
        s_up = jnp.concatenate([h[i] for h in up_total for i in range(2)], axis=1)
        s_down = jnp.concatenate([h.reshape(-1, D) for h in down_total])
    else:
        both = jnp.stack([h.reshape(3, D, GROUPS, WIDE // 2) for h in (keep_qkv, send_qkv)], axis=3)
        both = both.reshape(3, D, D)
        fold_rows = jnp.concatenate([keep_2, send_2]).reshape(folds, FF // wide, block_rows, D)
        both = (
            jnp.concatenate([both[0], both[1], both[2]], axis=1),
            jnp.concatenate([keep_o, send_o], axis=1),
            jnp.concatenate([h[i] for h in grads_1[::-1] for i in range(2)], axis=1),
            fold_rows.transpose(1, 0, 2, 3).reshape(FF, D),
        )
        s_joint, s_attn, s_up, s_down = [
            lax.psum_scatter(g.astype(f32), AXES, scatter_dimension=0, tiled=True) for g in both
        ]
        s_small = lax.psum_scatter(packed, AXES, scatter_dimension=0, tiled=True)[0]
    small_outs = []
    at = 0
    for g in grads:
        small_outs.append(s_small[at : at + g.shape[0] // n])
        at += g.shape[0] // n
    s_gain, s_shift, s_joint_bias, s_dy, s_up_bias = small_outs
    return (
        output,
        input_grad,
        s_gain,
        s_shift,
        s_joint,
        s_joint_bias,
        s_attn,
        s_dy,
        s_up,
        s_up_bias,
        s_down,
        s_dy,
    )


def solution(mesh):
    grid = Grid(mesh.shape["dp"], mesh.shape["fsdp"])
    rows2, rows1 = P(AXES, None), P(AXES)
    in_specs = (
        rows2,
        rows1,
        rows1,
        rows2,
        rows1,
        rows2,
        rows1,
        rows2,
        rows1,
        rows2,
        rows1,
        rows2,
        rows2,
        P(),
        P(),
    )
    out_specs = (
        rows2,
        rows2,
        rows1,
        rows1,
        rows2,
        rows1,
        rows2,
        rows1,
        rows2,
        rows1,
        rows2,
        rows1,
    )
    return jax.shard_map(
        functools.partial(shards, grid),
        mesh=mesh,
        in_specs=in_specs,
        out_specs=out_specs,
        check_vma=False,
    )
```

```python
import functools
import math

import jax
import jax.numpy as jnp
from jax import lax
from jax.experimental import pallas as pl
from jax.experimental.pallas import tpu as pltpu
from jax.sharding import PartitionSpec as P

D = 1024
HEADS = 16
HD = 64
ROT = 16
LEN = 1024
DOCS = 4
FF = 4096
AXES = ("dp", "fsdp")
BLOCK = 512

feature_scale = 0.2
epsilon = 1e-05
precise = lax.Precision.HIGHEST
bf16 = jnp.bfloat16
f32 = jnp.float32
VMEM_LIMIT = 60 << 20


def cost(flops, transcendentals, bytes_accessed):
    return pl.CostEstimate(
        flops=flops * 4, transcendentals=transcendentals, bytes_accessed=bytes_accessed * 4
    )


class Grid:
    def __init__(self, dp, fsdp):
        self.dp, self.fsdp = dp, fsdp
        rest = fsdp // 2
        self.nx = 4 if rest % 16 == 0 else 2
        self.nz = rest // self.nx
        self.ny = dp
        self.n = dp * fsdp
        self.sizes = {"y": self.ny, "z": self.nz, "x": self.nx, "c": 2}
        self.stride = {"y": fsdp, "z": self.nx * 2, "x": 2, "c": 1}

    def digits(self):
        y = lax.axis_index("dp")
        f = lax.axis_index("fsdp")
        return {"y": y, "z": f // (self.nx * 2), "x": (f // 2) % self.nx, "c": f % 2}

    def swap(self, value, digit, k):
        stride = self.stride[digit]
        size = self.sizes[digit]
        pairs = []
        for i in range(self.n):
            d = (i // stride) % size
            pairs.append((i, i + ((d ^ k) - d) * stride))
        return lax.ppermute(value, AXES, pairs)

    def swap_by_core(self, value, digit_0, digit_1):
        flips = (self.stride[digit_0], self.stride[digit_1])
        return lax.ppermute(value, AXES, [(i, i ^ flips[i % 2]) for i in range(self.n)])


def place(pieces, outs, moves, after=()):
    n_in = len(pieces)
    n_out = len(outs)

    def body(*refs):
        ins, rest = refs[:n_in], refs[n_in + len(after) :]
        res, held, sem, done = rest[:n_out], rest[n_out : 2 * n_out], rest[-2], rest[-1]
        copies = []
        for i, (src, src_at, dst, dst_at) in enumerate(moves):
            copies.append(
                pltpu.make_async_copy(ins[src].at[src_at()], held[dst].at[dst_at()], sem.at[i])
            )
        for copy in copies:
            copy.start()
        back = []
        for o in range(n_out):
            for copy, move in zip(copies, moves):
                if move[2] == o:
                    copy.wait()
            back.append(pltpu.make_async_copy(held[o], res[o], done.at[o]))
            back[-1].start()
        for copy in back:
            copy.wait()

    total = sum(math.prod(o.shape) * o.dtype.itemsize for o in outs)
    return pl.pallas_call(
        body,
        out_shape=tuple(outs),
        in_specs=[pl.BlockSpec(memory_space=pl.ANY)] * (n_in + len(after)),
        out_specs=tuple([pl.BlockSpec(memory_space=pl.ANY)] * n_out),
        scratch_shapes=[pltpu.VMEM(o.shape, o.dtype) for o in outs]
        + [pltpu.SemaphoreType.DMA((len(moves),)), pltpu.SemaphoreType.DMA((n_out,))],
        compiler_params=pltpu.CompilerParams(vmem_limit_bytes=VMEM_LIMIT),
        cost_estimate=cost(flops=0, transcendentals=0, bytes_accessed=2 * total),
        name="place",
    )(*pieces, *after)


class Gather:
    def __init__(self, grid, both, fields, after=()):
        if after:
            both, *_ = lax.optimization_barrier((both, *after))
        self.grid, self.fields = grid, fields
        self.shape, self.dt = both.shape, both.dtype
        self.pieces = [both] + [grid.swap(both, "z", k) for k in range(1, grid.nz)]

    def first(self):
        g = self.grid
        outs = [jax.ShapeDtypeStruct((g.nz,) + self.shape, self.dt)]
        moves = [
            (k, lambda: (slice(None),), 0, lambda k=k: (g.digits()["z"] ^ k,)) for k in range(g.nz)
        ]
        return self.pieces, outs, moves, self.after_first

    def after_first(self, placed):
        self.pieces = [placed[0], self.grid.swap_by_core(placed[0], "x", "y")]

    def second(self):
        g = self.grid
        outs = [jax.ShapeDtypeStruct((2, g.nz) + self.shape, self.dt)]

        def dst_at(k):
            d = g.digits()
            return (jnp.where(d["c"] == 0, d["x"], d["y"]) ^ k,)

        moves = [(k, lambda: (slice(None),), 0, lambda k=k: dst_at(k)) for k in range(2)]
        return self.pieces, outs, moves, self.after_second

    def after_second(self, placed):
        self.pieces = [placed[0], self.grid.swap_by_core(placed[0], "y", "x")]

    def cores(self, after=()):
        pieces = tuple(self.pieces)
        if after:
            pieces = lax.optimization_barrier((*pieces, *after))[:2]
        self.pieces = list(pieces) + [self.grid.swap(piece, "c", 1) for piece in pieces]

    def third(self):
        g, rows = self.grid, self.shape[1]
        outs, moves = [], []
        first = 0
        for o, (cols, blocks) in enumerate(self.fields):
            wide = cols // blocks
            split = blocks == 1
            outs.append(
                jax.ShapeDtypeStruct(
                    (2, g.nz, 2, 2, 1 if split else 2 * blocks, rows, 2 * wide if split else wide), self.dt
                )
            )
            for p in range(4):
                for d1 in range(2):
                    for b in range(blocks):
                        start = first + b * wide

                        def src_at(d1=d1, start=start, wide=wide):
                            return (d1, slice(None), slice(None), slice(None), pl.ds(start, wide))

                        def dst_at(p=p, d1=d1, b=b, wide=wide, split=split, blocks=blocks):
                            d = g.digits()
                            half = d["c"] ^ (p // 2)
                            d2 = jnp.where(half == 0, d["y"], d["x"]) ^ (p % 2)
                            y = jnp.where(half == 0, d2, d1)
                            x = jnp.where(half == 0, d1, d2)
                            block = 0 if split else half * blocks + b
                            at = pl.ds(pl.multiple_of(half * wide, wide), wide) if split else slice(None)
                            return (y, slice(None), x, slice(None), block, slice(None), at)

                        moves.append((p, src_at, o, dst_at))
            first += cols
        return self.pieces, outs, moves, self.after_third

    def after_third(self, placed):
        self.full = [w.reshape(-1, w.shape[-1]) for w in placed]


def pack(grid, groups):
    core = grid.digits()["c"]
    halves = [[], []]
    for group in groups:
        for shard, _ in group:
            middle = shard.shape[1] // 2
            halves[0].append(shard[:, :middle])
            halves[1].append(shard[:, middle:])
    low, high = [jnp.concatenate(h, axis=1) for h in halves]
    mine, other = jnp.where(core == 0, low, high), jnp.where(core == 0, high, low)
    got = grid.swap(other, "c", 1)
    both = jnp.stack([jnp.where(core == 0, mine, got), jnp.where(core == 0, got, mine)])
    result = []
    at = 0
    for group in groups:
        cols = sum(shard.shape[1] // 2 for shard, _ in group)
        result.append((both[:, :, at : at + cols], [(s.shape[1] // 2, max(1, b // 2)) for s, b in group]))
        at += cols
    return result


def place_all(plans, after=()):
    pieces, outs, moves = [], [], []
    for p, o, m, _ in plans:
        moves += [(len(pieces) + src, src_at, len(outs) + dst, dst_at) for src, src_at, dst, dst_at in m]
        pieces += p
        outs += o
    placed = place(pieces, outs, moves, after)
    at = 0
    for _, o, _, done in plans:
        done(placed[at : at + len(o)])
        at += len(o)
    return list(placed[:1])


TILE = 256
WIDE = 256
PER = WIDE // HD
STEPS = LEN // TILE
GROUPS = HEADS // PER
PAIRS = [(q, k) for q in range(STEPS) for k in range(max(0, q - 2), q + 1)]


def nn(a, b):
    return lax.dot_general(a, b, (((1,), (0,)), ((), ())), preferred_element_type=f32)


def nt(a, b):
    return lax.dot_general(a, b, (((1,), (1,)), ((), ())), preferred_element_type=f32)


def halves(v):
    high = v.astype(bf16)
    return high, (v - high.astype(f32)).astype(bf16)


ANYWHERE = pl.BlockSpec(memory_space=pl.ANY)


def once(shape):
    return pl.BlockSpec(shape, lambda *g: (0,) * len(shape), pipeline_mode=pl.Buffered(1))


def norm_body(x_ref, gain_ref, shift_ref, hid_ref, hid_t_ref):
    x = x_ref[...].astype(f32)
    center = x - jnp.mean(x, axis=-1, keepdims=True)
    inv = lax.rsqrt(jnp.mean(center * center, axis=-1, keepdims=True) + epsilon)
    hid = center * inv * gain_ref[...] + shift_ref[...]
    hid_ref[...] = hid.astype(bf16)
    hid_t_ref[...] = hid.T.astype(bf16)


def norm(tokens, gain, shift):
    return pl.pallas_call(
        norm_body,
        grid=(STEPS,),
        out_shape=(jax.ShapeDtypeStruct((LEN, D), bf16), jax.ShapeDtypeStruct((D, LEN), bf16)),
        in_specs=[pl.BlockSpec((TILE, D), lambda g: (g, 0)), once((1, D)), once((1, D))],
        out_specs=(
            pl.BlockSpec((TILE, D), lambda g: (g, 0)),
            pl.BlockSpec((D, TILE), lambda g: (0, g)),
        ),
        compiler_params=pltpu.CompilerParams(vmem_limit_bytes=VMEM_LIMIT),
        cost_estimate=cost(flops=1 << 25, transcendentals=0, bytes_accessed=6 << 20),
        name="norm",
    )(tokens, gain, shift)


def attention_body(
    n_carried,
    core_ref,
    hid_ref,
    hid_t_ref,
    dy_ref,
    wq_ref,
    wk_ref,
    wv_ref,
    bq_ref,
    bk_ref,
    bv_ref,
    wo_ref,
    cos_ref,
    left_ref,
    right_ref,
    proj_ref,
    proj_low_ref,
    ones_ref,
    quad_ref,
    doc_col_ref,
    doc_row_ref,
    *rest,
):
    (
        att_ref,
        dm_ref,
        keep_ref,
        send_ref,
        keep_o_ref,
        send_o_ref,
        sums_ref,
        mask,
        scores,
        yq,
        yk,
        fq,
        fk,
        val,
        val_h,
        fq_t,
        dnum,
        dnum_t,
        cross,
        cross_low,
        att_t,
        num,
        den,
        dfq,
        dfk_t,
        dv_t,
        eq,
        ek,
    ) = rest[n_carried:]
    span = [pl.ds(r * TILE, TILE) for r in range(STEPS)]
    lane = lax.broadcasted_iota(jnp.int32, (TILE, WIDE), 1) // HD
    ones = ones_ref[...]
    proj, proj_low = proj_ref[...], proj_low_ref[...]

    for i, (q, k) in enumerate(PAIRS):
        here = doc_col_ref[span[q], :] == doc_row_ref[:, span[k]]
        if q == k:
            row = lax.broadcasted_iota(jnp.int32, (TILE, TILE), 0)
            col = lax.broadcasted_iota(jnp.int32, (TILE, TILE), 1)
            here = here & (row >= col)
        mask[i] = jnp.where(here, 1.0, 0.0).astype(bf16)

    hid = hid_ref[...]
    val[...] = (nn(hid, wv_ref[...]) + bv_ref[...]).astype(bf16)
    eq[...] = nn(hid, wq_ref[...]) + bq_ref[...]
    ek[...] = nn(hid, wk_ref[...]) + bk_ref[...]
    for r in range(STEPS):
        for y_out, f_out, e_out, scale in ((yq, fq, eq, True), (yk, fk, ek, False)):
            raw = e_out[span[r], :]
            y = (
                raw * cos_ref[span[r], :]
                + pltpu.roll(raw, WIDE - 8, 1) * left_ref[span[r], :]
                + pltpu.roll(raw, 8, 1) * right_ref[span[r], :]
            )
            y_high, y_low = halves(y)
            s_high, s_low = halves(y * y)
            power = nt(y_high, proj) + nt(y_low, proj) + nt(y_high, proj_low)
            power = power - 0.5 * (nn(s_high, ones) + nn(s_low, ones))
            feat = jnp.exp(power)
            if scale:
                feat = feat * quad_ref[...]
            y_out[span[r], :] = y
            e_out[span[r], :] = feat
            f_out[span[r], :] = feat.astype(bf16)
            if scale:
                fq_t[:, span[r]] = feat.T.astype(bf16)

    def forward(h, carry):
        own = lane == h
        for r in range(STEPS):
            val_h[h, span[r], :] = jnp.where(own, val[span[r], :], jnp.ones((), bf16))
        total = None
        for i, (q, k) in enumerate(PAIRS):
            query = jnp.where(own, fq[span[q], :], jnp.zeros((), bf16))
            tile = nt(query, fk[span[k], :]).astype(bf16) * mask[i]
            scores[h * len(PAIRS) + i] = tile
            part = nn(tile, val_h[h, span[k], :])
            total = part if total is None else total + part
            if k == q:
                num[span[q], :] = jnp.where(own, total, num[span[q], :])
                den[span[q], :] = jnp.where(own, pltpu.roll(total, HD, 1), den[span[q], :])
                total = None
        return carry

    lax.fori_loop(0, PER, forward, 0, unroll=True)

    dfq[...] = nt(dy_ref[...], wo_ref[...])
    for r in range(STEPS):
        grad = dfq[span[r], :]
        inv = 1.0 / den[span[r], :]
        att = num[span[r], :] * inv
        att_ref[span[r], :] = att.astype(bf16)
        d_num = grad * inv
        dnum[span[r], :] = d_num.astype(bf16)
        dnum_t[:, span[r]] = d_num.T.astype(bf16)
        att_t[:, span[r]] = att.T.astype(bf16)
        high, low = halves(pltpu.roll(-d_num * att, HD, 1))
        cross[span[r], :] = high
        cross_low[span[r], :] = pltpu.roll(low.astype(f32), HD, 1).astype(bf16)

    def backward(h, carry):
        own = lane == h
        after = lane == lax.rem(h + 1, PER)
        later = lane == lax.rem(h + 2, PER)
        mine = pl.ds(pl.multiple_of(h * HD, HD), HD)
        dfk_t[mine, :] = jnp.zeros((HD, LEN), f32)
        dv_t[mine, :] = jnp.zeros((HD, LEN), f32)
        total = None
        for i, (q, k) in enumerate(PAIRS):
            left = jnp.where(
                own,
                dnum[span[q], :],
                jnp.where(
                    after,
                    cross[span[q], :],
                    jnp.where(later, cross_low[span[q], :], jnp.zeros((), bf16)),
                ),
            )
            tile = nt(left, val_h[h, span[k], :]).astype(bf16) * mask[i]
            part = nn(tile, fk[span[k], :])
            total = part if total is None else total + part
            dfk_t[mine, span[k]] += nn(fq_t[mine, span[q]], tile)
            dv_t[mine, span[k]] += nn(dnum_t[mine, span[q]], scores[h * len(PAIRS) + i])
            if k == q:
                dfq[span[q], :] = jnp.where(own, total, dfq[span[q], :])
                total = None
        return carry

    lax.fori_loop(0, PER, backward, 0, unroll=True)

    sums = [jnp.zeros((1, WIDE), f32)] * 3
    for r in range(STEPS):
        grads = []
        for d_feat, feat, y in (
            (dfq[span[r], :], eq, yq),
            (dfk_t[:, span[r]].T, ek, yk),
        ):
            e_high, e_low = halves(d_feat * feat[span[r], :])
            d_y = nn(e_high, proj) + nn(e_low, proj) + nn(e_high, proj_low)
            d_y = d_y - (nn(e_high, ones) + nn(e_low, ones)) * y[span[r], :]
            grads.append(
                d_y * cos_ref[span[r], :]
                - pltpu.roll(d_y, WIDE - 8, 1) * left_ref[span[r], :]
                - pltpu.roll(d_y, 8, 1) * right_ref[span[r], :]
            )
        grads.append(dv_t[:, span[r]].T)
        for i in range(3):
            low = grads[i].astype(bf16)
            dm_ref[i, span[r], :] = low
            sums[i] = sums[i] + jnp.sum(low.astype(f32), axis=0, keepdims=True)
    for i in range(3):
        sums_ref[pl.ds(i, 1), :] = sums[i]

    first = core_ref[0] == 0
    half = WIDE // 2
    for i in range(3):
        full = nn(hid_t_ref[...], dm_ref[i]).astype(bf16)
        low, high = full[:, :half], full[:, half:]
        keep_ref[i] = jnp.where(first, low, high)
        send_ref[i] = jnp.where(first, high, low)
    full = nn(att_t[...], dy_ref[...]).astype(bf16)
    low, high = full[:, : D // 2], full[:, D // 2 :]
    keep_o_ref[...] = jnp.where(first, low, high)
    send_o_ref[...] = jnp.where(first, high, low)


def attention(core, group, operands, w_qkv, w_out, carried, after):
    hid, hid_t, dy, b_qkv, cos_t, left_t, right_t, proj, proj_low, ones, quad, doc_col, doc_row = operands
    half = D // 2
    at = lambda shape, index: pl.BlockSpec(shape, lambda s: index, pipeline_mode=pl.Buffered(1))
    col = lambda part: at((D, WIDE), (0, part * 2 + group % 2))
    bias = lambda part: at((1, WIDE), (0, part * GROUPS + group))
    shapes = [
        ((LEN, D), bf16, at((LEN, WIDE), (0, group))),
        ((3, LEN, D), bf16, at((3, LEN, WIDE), (0, 0, group))),
        ((3, D, half), bf16, at((3, D, WIDE // 2), (0, 0, group))),
        ((3, D, half), bf16, at((3, D, WIDE // 2), (0, 0, group))),
        ((D, half), bf16, at((WIDE, half), (group, 0))),
        ((D, half), bf16, at((WIDE, half), (group, 0))),
        ((8, D), f32, at((8, WIDE), (0, group))),
    ]
    in_specs = [
        pl.BlockSpec(memory_space=pltpu.SMEM),
        once((LEN, D)),
        once((D, LEN)),
        once((LEN, D)),
        col(0),
        col(1),
        col(2),
        bias(0),
        bias(1),
        bias(2),
        at((WIDE, D), (group, 0)),
        once((LEN, WIDE)),
        once((LEN, WIDE)),
        once((LEN, WIDE)),
        once((WIDE, WIDE)),
        once((WIDE, WIDE)),
        once((WIDE, WIDE)),
        once((1, WIDE)),
        once((LEN, 1)),
        once((1, LEN)),
    ]
    extra = list(carried) + list(after)
    vm = pltpu.VMEM
    tall, flat = (LEN, WIDE), (WIDE, LEN)
    scratch = [
        vm((len(PAIRS), TILE, TILE), bf16),
        vm((PER * len(PAIRS), TILE, TILE), bf16),
        vm(tall, f32),
        vm(tall, f32),
        vm(tall, bf16),
        vm(tall, bf16),
        vm(tall, bf16),
        vm((PER,) + tall, bf16),
        vm(flat, bf16),
        vm(tall, bf16),
        vm(flat, bf16),
        vm(tall, bf16),
        vm(tall, bf16),
        vm(flat, bf16),
        vm(tall, f32),
        vm(tall, f32),
        vm(tall, f32),
        vm(flat, f32),
        vm(flat, f32),
        vm(tall, f32),
        vm(tall, f32),
    ]
    return pl.pallas_call(
        functools.partial(attention_body, len(extra)),
        grid=(1,),
        out_shape=tuple(jax.ShapeDtypeStruct(s, t) for s, t, _ in shapes),
        in_specs=in_specs + [ANYWHERE] * len(extra),
        out_specs=tuple(spec for _, _, spec in shapes),
        scratch_shapes=scratch,
        input_output_aliases={len(in_specs) + i: i for i in range(len(carried))},
        compiler_params=pltpu.CompilerParams(vmem_limit_bytes=VMEM_LIMIT),
        cost_estimate=cost(flops=30 << 30, transcendentals=0, bytes_accessed=20 << 20),
        name="attention",
    )(
        core, hid, hid_t, dy, w_qkv, w_qkv, w_qkv, b_qkv, b_qkv, b_qkv, w_out,
        cos_t, left_t, right_t, proj, proj_low, ones, quad, doc_col, doc_row, *extra,
    )


CALLS = 2


def up_body(rows, wide, n_extra, core_ref, hid_ref, dy_ref, w1_ref, b1_ref, *rest):
    act_ref, slope_ref, keep_ref, send_ref, act_t = rest[n_extra:]
    block = w1_ref.shape[1]
    for r in range(STEPS):
        at = pl.ds(r * TILE, TILE)
        upper = nn(hid_ref[at, :], w1_ref[...]) + b1_ref[...]
        bell = jnp.exp(-0.5 * upper * upper)
        phi = 0.5 + 0.5 * lax.erf(upper * (1.0 / math.sqrt(2.0)))
        act = (upper * phi).astype(bf16)
        act_ref[at, :] = act
        act_t[:, at] = act.T
        slope_ref[at, :] = (phi + upper * bell * (1.0 / math.sqrt(2.0 * math.pi))).astype(bf16)
    first = core_ref[0] == 0
    full = nn(act_t[...], dy_ref[...]).astype(bf16)
    top = wide // rows // 2
    for p in range(block // wide):
        for b in range(top):
            low = full[p * wide + b * rows : p * wide + (b + 1) * rows]
            start = p * wide + (top + b) * rows
            high = full[start : start + rows]
            keep_ref[b, pl.ds(p * rows, rows), :] = jnp.where(first, low, high)
            send_ref[b, pl.ds(p * rows, rows), :] = jnp.where(first, high, low)


def up_part(core, rows, wide, call, hid, dy, w1, b1, carried=(), after=()):
    grid = FF // BLOCK // CALLS
    base = call * grid
    top = wide // rows // 2
    per = BLOCK // wide * rows
    total = FF // wide * rows
    grad = ((top, total, D), bf16, pl.BlockSpec((top, per, D), lambda g: (0, base + g, 0)))
    units = ((LEN, FF), bf16, pl.BlockSpec((LEN, BLOCK), lambda g: (0, base + g)))
    shapes = [units, units, grad, grad]
    extra = list(carried) + list(after)
    return pl.pallas_call(
        functools.partial(up_body, rows, wide, len(extra)),
        grid=(grid,),
        out_shape=tuple(jax.ShapeDtypeStruct(s, t) for s, t, _ in shapes),
        in_specs=[
            pl.BlockSpec(memory_space=pltpu.SMEM),
            once((LEN, D)),
            once((LEN, D)),
            pl.BlockSpec((D, BLOCK), lambda g: (0, base + g)),
            pl.BlockSpec((1, BLOCK), lambda g: (0, base + g)),
        ]
        + [ANYWHERE] * len(extra),
        out_specs=tuple(spec for _, _, spec in shapes),
        scratch_shapes=[pltpu.VMEM((BLOCK, LEN), bf16)],
        input_output_aliases={5 + i: i for i in range(len(carried))},
        compiler_params=pltpu.CompilerParams(vmem_limit_bytes=VMEM_LIMIT),
        cost_estimate=cost(
            flops=4 * LEN * D * FF // CALLS, transcendentals=0, bytes_accessed=18 << 20
        ),
        name="up",
    )(core, hid, dy, w1, b1, *extra)


def down_body(n_extra, core_ref, hid_t_ref, dy_ref, w2_ref, slope_ref, *rest):
    dup_ref, sums_ref, grad_ref = rest[n_extra:]
    block = w2_ref.shape[0]
    total = jnp.zeros((1, block), f32)
    for r in range(STEPS):
        at = pl.ds(r * TILE, TILE)
        d_up = (nt(dy_ref[at, :], w2_ref[...]) * slope_ref[at, :].astype(f32)).astype(bf16)
        dup_ref[at, :] = d_up
        total = total + jnp.sum(d_up.astype(f32), axis=0, keepdims=True)
    sums_ref[...] = total
    grad_ref[0] = nn(hid_t_ref[...], dup_ref[...]).astype(bf16)


def down_part(core, call, hid_t, dy, w2, slope, carried=(), after=()):
    grid = FF // BLOCK // CALLS
    per = D // BLOCK
    unit = lambda g, ref: (ref[0] ^ 1 ^ call) * grid + g
    shapes = [
        ((LEN, FF), bf16, pl.BlockSpec((LEN, BLOCK), lambda g, ref: (0, unit(g, ref)))),
        ((1, FF), f32, pl.BlockSpec((1, BLOCK), lambda g, ref: (0, unit(g, ref)))),
        (
            (FF // D // CALLS, D, D),
            bf16,
            pl.BlockSpec((1, D, BLOCK), lambda g, ref: (g // per, 0, g % per)),
        ),
    ]
    extra = list(carried) + list(after)
    return pl.pallas_call(
        functools.partial(down_body, len(extra)),
        grid_spec=pltpu.PrefetchScalarGridSpec(
            num_scalar_prefetch=1,
            grid=(grid,),
            in_specs=[
                once((D, LEN)),
                once((LEN, D)),
                pl.BlockSpec((BLOCK, D), lambda g, ref: (unit(g, ref), 0)),
                pl.BlockSpec((LEN, BLOCK), lambda g, ref: (0, unit(g, ref))),
            ]
            + [ANYWHERE] * len(extra),
            out_specs=tuple(spec for _, _, spec in shapes),
        ),
        out_shape=tuple(jax.ShapeDtypeStruct(s, t) for s, t, _ in shapes),
        input_output_aliases={5 + i: i for i in range(len(carried))},
        compiler_params=pltpu.CompilerParams(vmem_limit_bytes=VMEM_LIMIT),
        cost_estimate=cost(
            flops=4 * LEN * D * FF // CALLS, transcendentals=0, bytes_accessed=18 << 20
        ),
        name="down",
    )(core, hid_t, dy, w2, slope, *extra)


CHUNK = 512


def output_first_body(n_after, act_ref, w2_ref, x_ref, bias_ref, *rest):
    out_ref = rest[n_after]

    @pl.when(pl.program_id(0) == 0)
    def _():
        out_ref[...] = x_ref[...].astype(f32) + bias_ref[...]

    out_ref[...] += nn(act_ref[...], w2_ref[...])


def output_first(act, w2, tokens, bias, after=()):
    return pl.pallas_call(
        functools.partial(output_first_body, len(after)),
        grid=(FF // CHUNK // 2,),
        out_shape=jax.ShapeDtypeStruct((LEN, D), f32),
        in_specs=[
            pl.BlockSpec((LEN, CHUNK), lambda g: (0, g)),
            pl.BlockSpec((CHUNK, D), lambda g: (g, 0)),
            once((LEN, D)),
            once((1, D)),
        ]
        + [ANYWHERE] * len(after),
        out_specs=once((LEN, D)),
        compiler_params=pltpu.CompilerParams(vmem_limit_bytes=VMEM_LIMIT),
        cost_estimate=cost(
            flops=LEN * D * FF, transcendentals=0, bytes_accessed=14 << 20
        ),
        name="output_first",
    )(act, w2, tokens, bias, *after)


def output_rest_body(n_after, act_ref, att_ref, w2_ref, wo_ref, acc_ref, *rest):
    out_ref = rest[n_after]
    step = pl.program_id(0)

    @pl.when(step == 0)
    def _():
        out_ref[...] = acc_ref[...] + nn(act_ref[...], w2_ref[...])

    @pl.when((step > 0) & (step < FF // CHUNK // 2))
    def _():
        out_ref[...] += nn(act_ref[...], w2_ref[...])

    @pl.when(step >= FF // CHUNK // 2)
    def _():
        out_ref[...] += nn(att_ref[...], wo_ref[...])


def output_rest(act, att, w2, wo, acc, after=()):
    lead, tail = FF // CHUNK // 2, D // CHUNK
    low = lambda g: lead + jnp.minimum(g, lead - 1)
    high = lambda g: jnp.maximum(g - lead, 0)
    return pl.pallas_call(
        functools.partial(output_rest_body, len(after)),
        grid=(lead + tail,),
        out_shape=jax.ShapeDtypeStruct((LEN, D), f32),
        in_specs=[
            pl.BlockSpec((LEN, CHUNK), lambda g: (0, low(g))),
            pl.BlockSpec((LEN, CHUNK), lambda g: (0, high(g))),
            pl.BlockSpec((CHUNK, D), lambda g: (low(g), 0)),
            pl.BlockSpec((CHUNK, D), lambda g: (high(g), 0)),
            once((LEN, D)),
        ]
        + [ANYWHERE] * len(after),
        out_specs=once((LEN, D)),
        compiler_params=pltpu.CompilerParams(vmem_limit_bytes=VMEM_LIMIT),
        cost_estimate=cost(
            flops=LEN * D * (FF + 2 * D), transcendentals=0, bytes_accessed=18 << 20
        ),
        name="output_rest",
    )(act, att, w2, wo, acc, *after)


def back_body(n_after, dup_ref, w1_ref, *rest):
    acc_ref = rest[n_after]
    step = pl.program_id(0)

    @pl.when(step == 0)
    def _():
        acc_ref[...] = nt(dup_ref[...], w1_ref[...])

    @pl.when(step > 0)
    def _():
        acc_ref[...] += nt(dup_ref[...], w1_ref[...])


def back_part(d_up, w1, after=()):
    return pl.pallas_call(
        functools.partial(back_body, len(after)),
        grid=(FF // CHUNK,),
        out_shape=jax.ShapeDtypeStruct((LEN, D), f32),
        in_specs=[
            pl.BlockSpec((LEN, CHUNK), lambda g: (0, g)),
            pl.BlockSpec((D, CHUNK), lambda g: (0, g)),
        ]
        + [ANYWHERE] * len(after),
        out_specs=once((LEN, D)),
        compiler_params=pltpu.CompilerParams(vmem_limit_bytes=VMEM_LIMIT),
        cost_estimate=cost(
            flops=2 * LEN * D * FF, transcendentals=0, bytes_accessed=20 << 20
        ),
        name="back",
    )(d_up, w1, *after)


def input_body(n_after, dm_ref, wa_ref, wb_ref, acc_ref, x_ref, cot_ref, gain_ref, *rest):
    out_ref, sums_ref, acc = rest[n_after:]
    step = pl.program_id(0)
    last = 3 * D // CHUNK - 1

    @pl.when(step == 0)
    def _():
        acc[...] = acc_ref[...] + nt(dm_ref[0], wa_ref[...])

    @pl.when((step > 0) & (step < 3))
    def _():
        acc[...] += nt(dm_ref[0], wa_ref[...])

    @pl.when(step >= 3)
    def _():
        acc[...] += nt(dm_ref[0], wb_ref[...])

    @pl.when(step == last)
    def _():
        g_gain, g_shift = jnp.zeros((1, D), f32), jnp.zeros((1, D), f32)
        for r in range(STEPS):
            at = pl.ds(r * TILE, TILE)
            x = x_ref[at, :].astype(f32)
            center = x - jnp.mean(x, axis=-1, keepdims=True)
            inv = lax.rsqrt(jnp.mean(center * center, axis=-1, keepdims=True) + epsilon)
            normed = center * inv
            d_hidden = acc[at, :]
            g_gain = g_gain + jnp.sum(d_hidden * normed, axis=0, keepdims=True)
            g_shift = g_shift + jnp.sum(d_hidden, axis=0, keepdims=True)
            d_normed = d_hidden * gain_ref[...]
            mean_grad = jnp.mean(d_normed, axis=-1, keepdims=True)
            mean_cross = jnp.mean(d_normed * normed, axis=-1, keepdims=True)
            out_ref[at, :] = cot_ref[at, :] + inv * (d_normed - mean_grad - normed * mean_cross)
        sums_ref[0:1, :] = g_gain
        sums_ref[1:2, :] = g_shift


def input_part(d_mixed, wa, wb, acc, tokens, cotangent, gain, after=()):
    per = D // CHUNK
    return pl.pallas_call(
        functools.partial(input_body, len(after)),
        grid=(3 * per,),
        out_shape=(jax.ShapeDtypeStruct((LEN, D), f32), jax.ShapeDtypeStruct((8, D), f32)),
        in_specs=[
            pl.BlockSpec((1, LEN, CHUNK), lambda g: (g % 3, 0, g // 3)),
            pl.BlockSpec((D, CHUNK), lambda g: (0, jnp.minimum(g, 2))),
            pl.BlockSpec((D, CHUNK), lambda g: (0, jnp.maximum(g - 3, 0))),
            once((LEN, D)),
            once((LEN, D)),
            once((LEN, D)),
            once((1, D)),
        ]
        + [ANYWHERE] * len(after),
        out_specs=(once((LEN, D)), once((8, D))),
        scratch_shapes=[pltpu.VMEM((LEN, D), f32)],
        compiler_params=pltpu.CompilerParams(vmem_limit_bytes=VMEM_LIMIT),
        cost_estimate=cost(
            flops=6 * LEN * D * D, transcendentals=0, bytes_accessed=32 << 20
        ),
        name="input",
    )(d_mixed, wa, wb, acc, tokens, cotangent, gain, *after)


def fold(terms, view, block, in_at, out_view, out_block, out_at, n, steps, scalars, after=()):
    args, in_specs, out_specs, shapes, plan = [], [], [], [], []
    count = sum(part.shape[0] for part in terms[0])
    for j in range(n):
        sources = []
        for term in terms:
            spans = []
            at = 0
            for part in term:
                k = part.shape[0]
                spans.append((len(args), at, k))
                args.append(part.reshape((k,) + view))
                in_specs.append(
                    pl.BlockSpec((k,) + block, lambda s, ref, j=j: (0,) + in_at(s, j, ref))
                )
                at += k
            sources.append(spans)
        plan.append(sources)
        out_specs.append(pl.BlockSpec((count,) + out_block, lambda s, ref: (0,) + out_at(s)))
        shapes.append(jax.ShapeDtypeStruct((count,) + out_view, bf16))
    n_args = len(args)
    n_after = len(after)
    moved = n * (len(terms) + 1) * 2 * count * math.prod(out_view)

    def body(ref, *refs):
        for o, sources in enumerate(plan):
            out = refs[n_args + n_after + o]
            cuts = sorted({cut for spans in sources for _, at, k in spans for cut in (at, at + k)})
            for lo, hi in zip(cuts, cuts[1:]):
                total = None
                for spans in sources:
                    for arg, at, k in spans:
                        if at <= lo and hi <= at + k:
                            value = refs[arg][lo - at : hi - at]
                            total = value if total is None else total + value
                out[lo:hi] = total.reshape((hi - lo,) + out_block)

    return list(
        pl.pallas_call(
            body,
            grid_spec=pltpu.PrefetchScalarGridSpec(
                num_scalar_prefetch=1,
                grid=(steps,),
                in_specs=in_specs + [ANYWHERE] * n_after,
                out_specs=out_specs,
            ),
            out_shape=tuple(shapes),
            compiler_params=pltpu.CompilerParams(vmem_limit_bytes=VMEM_LIMIT),
            cost_estimate=cost(flops=moved, transcendentals=0, bytes_accessed=moved),
            name="fold",
        )(scalars, *args, *after)
    )


class Reduction:
    def __init__(self, grid, keep, send):
        self.grid = grid
        self.d = d = grid.digits()
        first = d["c"] == 0
        self.own = jnp.where(first, d["x"], d["y"]).astype(jnp.int32)
        self.next = jnp.where(first, d["y"], d["x"]).astype(jnp.int32)
        self.cols = keep[0].shape[-1]
        self.rows = keep[0].shape[1] // grid.n
        self.terms = [keep, [grid.swap(v, "c", 1) for v in send]]

    def token(self):
        return self.terms[0]

    def first(self, after=()):
        g, cols, two = self.grid, self.cols, 2 * self.rows
        half = cols // 2

        def in_at(s, j, ref):
            mine, other = ref[1] ^ j, s // 2
            y = jnp.where(ref[0] == 0, other, mine)
            x = jnp.where(ref[0] == 0, mine, other)
            return (y, 0, x, 0, s % 2)

        parts = fold(
            self.terms,
            (2, g.nz, 2, two, cols),
            (1, g.nz, 1, two, half),
            in_at,
            (2, g.nz, two, cols),
            (1, g.nz, two, half),
            lambda s: (s // 2, 0, 0, s % 2),
            2,
            4,
            jnp.stack([self.d["c"].astype(jnp.int32), self.own]),
            after,
        )
        self.terms = [parts[:1], [g.swap_by_core(parts[1], "x", "y")]]

    def second(self, after=()):
        g, cols, two = self.grid, self.cols, 2 * self.rows
        part = cols // 4
        parts = fold(
            self.terms,
            (2, g.nz, two, cols),
            (1, g.nz, two, part),
            lambda s, j, ref: (ref[0] ^ j, 0, 0, s),
            (g.nz, two, cols),
            (g.nz, two, part),
            lambda s: (0, 0, s),
            2,
            4,
            self.next[None],
            after,
        )
        self.terms = [parts[:1], [g.swap_by_core(parts[1], "y", "x")]]

    def third(self, after=()):
        g, cols, two = self.grid, self.cols, 2 * self.rows
        part = cols // 2
        parts = fold(
            self.terms,
            (g.nz, two, cols),
            (1, two, part),
            lambda s, j, ref: (ref[0] ^ j, 0, s),
            (two, cols),
            (two, part),
            lambda s: (0, s),
            g.nz,
            2,
            self.d["z"].astype(jnp.int32)[None],
            after,
        )
        self.parts = [parts[0]] + [g.swap(parts[j], "z", j) for j in range(1, g.nz)]

    def settle(self, after=()):
        if after:
            self.parts = lax.optimization_barrier((*self.parts, *after))[: len(self.parts)]
        total = self.parts[0].astype(f32)
        for part in self.parts[1:]:
            total = total + part.astype(f32)
        self.total = total.reshape(-1, 2, self.rows, self.cols)

    def result(self, after=()):
        total = self.total
        if after:
            total = lax.optimization_barrier((total, *after))[0]
        core = self.d["c"]
        mine = pick(total, 1, core)
        got = self.grid.swap(pick(total, 1, 1 - core), "c", 1)
        return jnp.where(core == 0, mine, got), jnp.where(core == 0, got, mine)


class SmallReduction:
    def __init__(self, grid, grad):
        self.grid = grid
        self.d = grid.digits()
        self.now = grad.reshape(grid.ny, grid.nz, grid.nx, 2, grad.shape[1])

    def step(self, digit, axis, after=None):
        if after is not None:
            self.now, _ = lax.optimization_barrier((self.now, after))
        mine = pick(self.now, axis, self.d[digit])
        for k in range(1, self.grid.sizes[digit]):
            mine = mine + self.grid.swap(pick(self.now, axis, self.d[digit] ^ k), digit, k)
        self.now = mine


def tables(node_seeds, node_weights):
    width = node_seeds.shape[1]
    uniform_pts = (node_seeds.astype(jnp.float32) + 0.5) / 1024.0
    nodes = math.sqrt(2.0) * lax.erf_inv(2.0 * uniform_pts - 1.0)
    order = jnp.arange(width).astype(jnp.float32)
    scales = jnp.where(order[:, None] == 0.0, math.sqrt(1.0 / width), math.sqrt(2.0 / width))
    basis = scales * jnp.cos(
        math.pi * (2.0 * order[None, :] + 1.0) * order[:, None] / (2.0 * width)
    )
    projection = jnp.dot(nodes, basis, precision=precise)
    weights_float = node_weights.astype(jnp.float32)
    return (projection, weights_float / jnp.sum(weights_float))


def layout(lengths):
    ends = jnp.cumsum(lengths)
    starts = ends - lengths
    places = jnp.arange(LEN, dtype=jnp.int32)
    doc_ids = jnp.sum((places[:, None] >= ends[None, :]).astype(jnp.int32), axis=1)
    owners = doc_ids[:, None] == jnp.arange(DOCS, dtype=jnp.int32)[None, :]
    begins = jnp.sum(jnp.where(owners, starts[None, :], 0), axis=1)
    return (doc_ids, (places - begins).astype(jnp.float32))


def rotary(positions):
    half_rot = ROT // 2
    freqs = 10000.0 ** (-2.0 * jnp.arange(half_rot).astype(jnp.float32) / ROT)
    angles = positions[:, None] * freqs[None, :]
    return (jnp.cos(angles), jnp.sin(angles))


def pick(value, axis, index):
    return lax.dynamic_index_in_dim(value, index, axis, keepdims=False)


def shards(
    grid,
    tokens,
    ln_gain,
    ln_bias,
    qkv_weight,
    qkv_bias,
    out_weight,
    out_bias,
    fc1_weight,
    fc1_bias,
    fc2_weight,
    fc2_bias,
    cotangent,
    doc_lengths,
    node_seeds,
    node_weights,
):
    n = grid.n
    rows = qkv_weight.shape[0]
    staged = rows % 32 == 0 and grid.nx == 2 and grid.ny == 2
    block_rows = rows if staged else 32
    wide = FF // n if staged else 64
    folds = wide // block_rows
    vectors = (ln_gain, ln_bias, qkv_bias, out_bias, fc1_bias, fc2_bias)
    small = jnp.concatenate(vectors)
    per_row = small.shape[0] // rows
    small = jnp.pad(small.reshape(rows, per_row), ((0, 0), (0, 128 - per_row)))
    dy_low = cotangent.astype(bf16)
    dy_sums = jnp.sum(dy_low.astype(f32), axis=0)
    projection, quad = tables(node_seeds, node_weights)
    doc_ids, positions = layout(doc_lengths[0])
    cos, sin = rotary(positions)
    flat = jnp.ones((LEN, HD - ROT), f32)
    none = jnp.zeros((LEN, ROT // 2), f32)
    cos_t = feature_scale * jnp.tile(jnp.concatenate([cos, cos, flat], axis=1), (1, PER))
    left_t = feature_scale * jnp.tile(jnp.concatenate([-sin, none, 0 * flat], axis=1), (1, PER))
    right_t = feature_scale * jnp.tile(jnp.concatenate([none, sin, 0 * flat], axis=1), (1, PER))
    eye = jnp.eye(PER, dtype=f32)
    wide_proj = jnp.einsum("ab,jd->ajbd", eye, projection, precision=precise).reshape(WIDE, WIDE)
    near = lax.reduce_precision(wide_proj, 8, 7)
    ones = jnp.kron(eye, jnp.ones((HD, HD), f32)).astype(bf16)

    if staged:
        pairs = [
            jnp.concatenate([qkv_weight[:, p * D + h : p * D + h + D // 2] for p in range(3)], axis=1)
            for h in (0, D // 2)
        ]
        folded = fc2_weight.reshape(folds, rows, D)
        folded = jnp.concatenate([folded[i] for i in range(folds)], axis=1)
        packed = pack(
            grid,
            [
                [(pairs[0], 1), (out_weight, 1), (jnp.pad(small, ((0, 0), (0, 128))), 1)],
                [(pairs[1], 1)],
                [(fc1_weight, 1)],
                [(folded, folds)],
            ],
        )
        head = Gather(grid, *packed[0])
        token = place_all([head.first()])
        rest = Gather(grid, *packed[1], token)
        token = place_all([head.second(), rest.first()])
        fill = lax.optimization_barrier((dy_low, dy_sums, cos_t, left_t, right_t, near))
        dy_low, dy_sums, cos_t, left_t, right_t, near = fill
        head.cores(fill)
        token = place_all([head.third()])
        ups = Gather(grid, *packed[2], token)
        pair_weights, attn_weight, small_all = [head.full[0], None], head.full[1], head.full[2]
    else:
        joint_weight, small_all, attn_weight, up_weight, down_weight = [
            lax.all_gather(w, AXES, axis=0, tiled=True)
            for w in (qkv_weight, small, out_weight, fc1_weight, fc2_weight)
        ]
        pair_weights = [
            jnp.concatenate([joint_weight[:, p * D + h : p * D + h + D // 2] for p in range(3)], axis=1)
            for h in (0, D // 2)
        ]
    small_all = small_all[:, :per_row].reshape(n, rows * per_row)
    whole = []
    at = 0
    for v in vectors:
        whole.append(small_all[:, at : at + v.shape[0]].reshape(n * v.shape[0]).astype(f32))
        at += v.shape[0]
    norm_gain, norm_shift, joint_bias, attn_bias, up_bias, down_bias = whole

    core = grid.digits()["c"] if staged else jnp.zeros((), jnp.int32)
    core_arg = core.reshape(1).astype(jnp.int32)
    hidden_low, hidden_t = norm(tokens, norm_gain[None], norm_shift[None])

    operands = (
        hidden_low,
        hidden_t,
        dy_low,
        joint_bias[None],
        cos_t,
        left_t,
        right_t,
        near.astype(bf16),
        (wide_proj - near).astype(bf16),
        ones,
        jnp.tile(quad, PER)[None],
        doc_ids[:, None],
        doc_ids[None],
    )
    carried = ()
    for group in range(GROUPS):
        after = ()
        if staged and group == 1:
            after = place_all([rest.second(), ups.first()], carried[:1])
            downs = Gather(grid, *packed[3], after)
        if staged and group == 2:
            token = place_all([ups.second(), downs.first()], carried[:1])
            rest.cores(token)
            place_all([rest.third()], token)
            pair_weights[1] = rest.full[0]
        if staged and group == 3:
            after = place_all([downs.second()], carried[:1])
            ups.cores(carried[:1])
        carried = attention(
            core_arg, group, operands, pair_weights[group // 2], attn_weight, carried, after
        )
    att, d_mixed, keep_qkv, send_qkv, keep_o, send_o, joint_sums = carried
    after = carried[:1]
    if staged:
        joint_sum = Reduction(grid, [keep_qkv, keep_o[None]], [send_qkv, send_o[None]])
        after = place_all([ups.third()], carried[:1])
        up_weight = ups.full[0]
        downs.cores(carried[:1])
    hidden = ()
    for call in range(CALLS):
        if staged and call == 1:
            joint_sum.first(hidden[:1])
            after = place_all([downs.third()], joint_sum.token())
            (down_weight,) = downs.full
        hidden = up_part(
            core_arg, block_rows, wide, call, hidden_low, dy_low, up_weight, up_bias[None], hidden, after
        )
    act, slope, keep_2, send_2 = hidden
    after = hidden[:1]
    if staged:
        down_sum = Reduction(grid, [keep_2], [send_2])
        joint_sum.second(hidden[:1])
        after = joint_sum.token()
    back = ()
    grads_1 = []
    for call in range(CALLS):
        if staged and call == 1:
            joint_sum.third(back[:1])
            down_sum.first(joint_sum.parts[:1])
            after = down_sum.token()
        d_up, up_sums, grad = down_part(
            core_arg, call, hidden_t, dy_low, down_weight, slope, back, after
        )
        back = (d_up, up_sums)
        grads_1.append(grad)
    after = ()
    if staged:
        up_sum = Reduction(grid, grads_1[1:], grads_1[:1])
        joint_sum.settle(back[:1])
        down_sum.second(back[:1])
        after = down_sum.token() + [joint_sum.total]
    d_hidden = back_part(d_up, up_weight, after)
    bias = (attn_bias + down_bias)[None]
    g_up_bias = up_sums.reshape(FF)
    g_joint_bias = joint_sums[:3].reshape(3 * D)
    after = ()
    if staged:
        up_sum.first([d_hidden])
        down_sum.third(up_sum.token())
        after = down_sum.parts[:1]
    input_grad, norm_sums = input_part(
        d_mixed, *pair_weights, d_hidden, tokens, cotangent, norm_gain[None], after
    )
    grads = (norm_sums[0], norm_sums[1], g_joint_bias, dy_sums, g_up_bias)
    packed = jnp.concatenate([g.reshape(n, -1) for g in grads], axis=1)
    after = ()
    if staged:
        down_sum.settle([input_grad])
        up_sum.second([input_grad, down_sum.total])
        token = up_sum.token()
        total, down_total = joint_sum.result(token), down_sum.result(token)
        packed, _ = lax.optimization_barrier((packed, token[0]))
        small_sum = SmallReduction(grid, packed)
        small_sum.step("z", 1)
        small_sum.step("x", 1)
        small_sum.step("y", 0)
        small_sum.step("c", 0)
        s_small = small_sum.now
        both = jnp.stack([h[:3].reshape(3, rows, GROUPS, WIDE // 2) for h in total], axis=3)
        both = both.reshape(3, rows, D)
        s_joint = jnp.concatenate([both[0], both[1], both[2]], axis=1)
        s_attn = jnp.concatenate([h[3] for h in total], axis=1)
        s_down = jnp.concatenate([h.reshape(-1, D) for h in down_total])
        s_small, s_joint, s_attn, s_down = lax.optimization_barrier((s_small, s_joint, s_attn, s_down))
        up_sum.third([s_small[None], s_joint, s_attn, s_down])
        after = up_sum.parts[:1]
    output = output_first(act, down_weight, tokens, bias, after)
    output = output_rest(act, att, down_weight, attn_weight, output)
    if staged:
        up_sum.settle([output])
        up_total = up_sum.result()
        s_up = jnp.concatenate([h[i] for h in up_total for i in range(2)], axis=1)
    else:
        both = jnp.stack([h.reshape(3, D, GROUPS, WIDE // 2) for h in (keep_qkv, send_qkv)], axis=3)
        both = both.reshape(3, D, D)
        fold_rows = jnp.concatenate([keep_2, send_2]).reshape(folds, FF // wide, block_rows, D)
        both = (
            jnp.concatenate([both[0], both[1], both[2]], axis=1),
            jnp.concatenate([keep_o, send_o], axis=1),
            jnp.concatenate([h[i] for h in grads_1[::-1] for i in range(2)], axis=1),
            fold_rows.transpose(1, 0, 2, 3).reshape(FF, D),
        )
        s_joint, s_attn, s_up, s_down = [
            lax.psum_scatter(g.astype(f32), AXES, scatter_dimension=0, tiled=True) for g in both
        ]
        s_small = lax.psum_scatter(packed, AXES, scatter_dimension=0, tiled=True)[0]
    small_outs = []
    at = 0
    for g in grads:
        small_outs.append(s_small[at : at + g.shape[0] // n])
        at += g.shape[0] // n
    s_gain, s_shift, s_joint_bias, s_dy, s_up_bias = small_outs
    return (
        output,
        input_grad,
        s_gain,
        s_shift,
        s_joint,
        s_joint_bias,
        s_attn,
        s_dy,
        s_up,
        s_up_bias,
        s_down,
        s_dy,
    )


def solution(mesh):
    grid = Grid(mesh.shape["dp"], mesh.shape["fsdp"])
    rows2, rows1 = P(AXES, None), P(AXES)
    in_specs = (
        rows2,
        rows1,
        rows1,
        rows2,
        rows1,
        rows2,
        rows1,
        rows2,
        rows1,
        rows2,
        rows1,
        rows2,
        rows2,
        P(),
        P(),
    )
    out_specs = (
        rows2,
        rows2,
        rows1,
        rows1,
        rows2,
        rows1,
        rows2,
        rows1,
        rows2,
        rows1,
        rows2,
        rows1,
    )
    return jax.shard_map(
        functools.partial(shards, grid),
        mesh=mesh,
        in_specs=in_specs,
        out_specs=out_specs,
        check_vma=False,
    )
```
